128 devices in a mesh: row: 16 (over x, y_lo, core), col: 8 (over z, y_hi).
Axes of the slice: x: 4, y: 4 (y_hi: 2, y_lo: 2; y = y_hi * 2 + y_lo), z: 4, core: 2. Of those that a mesh axis runs over, the one named last changes fastest.
Arguments:
- block_out: bfloat16 [768, 8192], P('row', 'col'), may hold values from -250 to 250
- stream_mid: bfloat16 [768, 8192], P('row', 'col'), may hold values from -250 to 250
- gate_pre: bfloat16 [768, 28672], P('row', 'col'), may hold values from -8 to 8
- up_pre: bfloat16 [768, 28672], P('row', 'col'), may hold values from -6 to 6
- final_gain: float32 [8192], P('col'), may hold values from 0.28 to 1.72
- mlp_gain: float32 [8192], P('col'), may hold values from 0.1 to 1.9
- value_weight: float32 [8192], P('col'), may hold values from -0.006629126 to 0.006629126
- returns: float32 [768], P('row'), may hold values from -6 to 6
- response_mask: int32 [768], P('row'), may hold values from 0 to 1, as said below
- w_gate: bfloat16 [8192, 28672], P('row', 'col'), may hold values from -0.0625 to 0.0625
- w_up: bfloat16 [8192, 28672], P('row', 'col'), may hold values from -0.0625 to 0.0625
- w_down: bfloat16 [28672, 8192], P('col', 'row'), may hold values from -0.03125 to 0.03125
Outputs:
- stream_mid_gradient: bfloat16 [768, 8192], P('row', 'col')
- d_w_down: float32 [28672, 8192], P('col', 'row')
The draws below stay inside these ranges and needn't reach their ends.
Inputs may be any that keep to these rules, and one draw needn't show every extreme that they name: `response_mask`: the last token of the micro-batch is a response token.
All inputs are finite; a program needn't handle non-finite values.
Results may differ from the reference program's by a relative error of at most 0.0075.
Values may be sent and summed in bfloat16 or wider, within the bound.
A program may use at most 128 MiB of HBM per device.

```python
import math
import jax
import jax.numpy as jnp
from jax import lax

MODEL_WIDTH = 8192
FF = 28672
TOKENS = 768


def head_parts(key):
    gain_key, weight_key = jax.random.split(jax.random.fold_in(key, 5), 2)
    gain_values = 1.0 + 0.18 * jnp.clip(jax.random.normal(gain_key, (MODEL_WIDTH,), jnp.float32), -4.0, 4.0)
    weight_normal = jnp.clip(jax.random.normal(weight_key, (MODEL_WIDTH,), jnp.float32), -4.0, 4.0)
    return (gain_values, weight_normal)


def draw_stream(key, along_head):
    base_key = jax.random.fold_in(key, 0)
    col_key = jax.random.fold_in(key, 1)
    row_key = jax.random.fold_in(key, 2)
    sign_key = jax.random.fold_in(key, 4)
    position = jnp.arange(MODEL_WIDTH, dtype=jnp.float32) / MODEL_WIDTH
    col_scale = 10.0 ** position * jax.random.uniform(col_key, (MODEL_WIDTH,), jnp.float32, 0.7, 1.4)
    noise = jnp.clip(jax.random.normal(base_key, (TOKENS, MODEL_WIDTH), jnp.float32), -4.0, 4.0)
    row_scale = jnp.exp(jax.random.uniform(row_key, (TOKENS,), jnp.float32, 0.0, math.log(10.0)))
    field = noise * col_scale[None, :] / 8.0
    sign = (2 * jax.random.randint(sign_key, (TOKENS,), 0, 2, dtype=jnp.int32) - 1).astype(jnp.float32)
    field = field + 0.5 * sign[:, None] * along_head[None, :]
    return jnp.clip(field * row_scale[:, None], -250.0, 250.0).astype(jnp.bfloat16)


def draw_block_out(key, part):
    gain_values, weight_normal = head_parts(key)
    return draw_stream(jax.random.fold_in(key, 11), gain_values * weight_normal)


def draw_stream_mid(key, part):
    return draw_stream(jax.random.fold_in(key, 23), jnp.zeros((MODEL_WIDTH,), jnp.float32))


def draw_final_gain(key, part):
    gain_values, weight_normal = head_parts(key)
    return gain_values.astype(jnp.float32)


def draw_value_weight(key, part):
    gain_values, weight_normal = head_parts(key)
    return (weight_normal * (0.15 / math.sqrt(MODEL_WIDTH))).astype(jnp.float32)


def draw_response_mask(key, part):
    position = jnp.arange(TOKENS, dtype=jnp.int32)
    limit = 200 + 600 * position // max(TOKENS - 1, 1)
    ticket = jax.random.randint(jax.random.fold_in(key, 37), (TOKENS,), 0, 1000, dtype=jnp.int32)
    marked = (ticket < limit).astype(jnp.int32)
    return jnp.where(position == TOKENS - 1, 1, marked).astype(jnp.int32)


def block_levels(own_key, shape, cuts, smallest, largest):
    factor_of = 1.0
    for axis_at, shards_of in cuts:
        draws = jax.random.uniform(jax.random.fold_in(jax.random.fold_in(own_key, 6), axis_at), (shards_of,), jnp.float32, smallest / len(cuts), largest / len(cuts))
        factor_of = factor_of * jnp.repeat(jnp.exp(draws), shape[axis_at] // shards_of).reshape((-1,) + (1,) * (len(shape) - 1 - axis_at))
    return factor_of


def centred(rng, shape, deviation, reach, shards=(), held_as=jnp.bfloat16):
    values = jax.random.normal(rng, shape, jnp.float32) * deviation
    if len(shards) > 0:
        values = block_levels(rng, shape, shards, -0.22, 0.18) * values
    return jnp.clip(values, min=-reach, max=reach).astype(held_as)


def setup_inputs(seed: int = 0) -> dict:
    arg_keys = jax.random.split(jax.random.key(seed), 13)
    block_out = draw_block_out(jax.random.fold_in(arg_keys[12], 71), 0)
    stream_mid = draw_stream_mid(jax.random.fold_in(arg_keys[12], 71), 0)
    gate_pre = centred(arg_keys[2], (TOKENS, FF), 2.0, 8.0, ((0, 16), (1, 8)))
    up_pre = centred(arg_keys[3], (TOKENS, FF), 1.0, 6.0, ((0, 16), (1, 8)))
    final_gain = draw_final_gain(jax.random.fold_in(arg_keys[12], 71), 0)
    mlp_gain = jnp.clip(1.0 + 0.18 * jax.random.normal(arg_keys[5], (MODEL_WIDTH,), jnp.float32), 0.1, 1.9)
    value_weight = draw_value_weight(jax.random.fold_in(arg_keys[12], 71), 0)
    returns = centred(arg_keys[7], (TOKENS,), 1.0, 6.0, ((0, 16),), jnp.float32)
    response_mask = draw_response_mask(jax.random.fold_in(arg_keys[12], 71), 0)
    w_gate = centred(arg_keys[9], (MODEL_WIDTH, FF), MODEL_WIDTH ** -0.5, 0.0625, ((0, 16), (1, 8)))
    w_up = centred(arg_keys[10], (MODEL_WIDTH, FF), MODEL_WIDTH ** -0.5, 0.0625, ((0, 16), (1, 8)))
    w_down = centred(arg_keys[11], (FF, MODEL_WIDTH), FF ** -0.5, 0.03125, ((0, 8), (1, 16)))
    return dict(block_out=block_out, stream_mid=stream_mid, gate_pre=gate_pre, up_pre=up_pre, final_gain=final_gain, mlp_gain=mlp_gain, value_weight=value_weight, returns=returns, response_mask=response_mask, w_gate=w_gate, w_up=w_up, w_down=w_down)


epsilon = 1e-05

def contract(left, right, left_dim, right_dim):
    return lax.dot_general(left, right, (((left_dim,), (right_dim,)), ((), ())), preferred_element_type=jnp.float32)

def reference(block_out, stream_mid, gate_pre, up_pre, final_gain, mlp_gain, value_weight, returns, response_mask, w_gate, w_up, w_down):
    output_widened = block_out.astype(jnp.float32)
    middle_widened = stream_mid.astype(jnp.float32)
    output_inverse_root = lax.rsqrt(lax.optimization_barrier(jnp.mean(output_widened * output_widened, axis=1)) + epsilon)
    output_normalized_rows = output_widened * output_inverse_root[:, None]
    value_head = final_gain * value_weight
    value_estimate = lax.optimization_barrier(jnp.sum(output_normalized_rows * value_head[None, :], axis=1))
    live = response_mask.astype(jnp.float32)
    count = jnp.sum(live)
    dvalue = live * (value_estimate - returns) * (TOKENS * math.sqrt(MODEL_WIDTH) / count)
    adjoint_vector = value_head[None, :] * dvalue[:, None]
    inner_product = lax.optimization_barrier(jnp.sum(adjoint_vector * output_normalized_rows, axis=1))
    output_gradient = (output_inverse_root[:, None] * (adjoint_vector - output_normalized_rows * (inner_product / MODEL_WIDTH)[:, None])).astype(jnp.bfloat16)
    gate_wide = gate_pre.astype(jnp.float32)
    up_wide = up_pre.astype(jnp.float32)
    sigmoid_gate = jax.nn.sigmoid(gate_wide)
    hidden = (gate_wide * sigmoid_gate * up_wide).astype(jnp.bfloat16)
    d_w_down = contract(hidden, output_gradient, 0, 0)
    d_hidden = contract(output_gradient, w_down, 1, 1)
    d_gate = (d_hidden * up_wide * sigmoid_gate * (1.0 + gate_wide * (1.0 - sigmoid_gate))).astype(jnp.bfloat16)
    d_up = (d_hidden * gate_wide * sigmoid_gate).astype(jnp.bfloat16)
    d_normed = contract(d_gate, w_gate, 1, 1) + contract(d_up, w_up, 1, 1)
    middle_inverse_root = lax.rsqrt(lax.optimization_barrier(jnp.mean(middle_widened * middle_widened, axis=1)) + epsilon)
    middle_normalized_rows = middle_widened * middle_inverse_root[:, None]
    scaled_rows = d_normed * mlp_gain[None, :]
    middle_inner_product = lax.optimization_barrier(jnp.sum(scaled_rows * middle_normalized_rows, axis=1))
    stream_mid_gradient = output_gradient.astype(jnp.float32) + middle_inverse_root[:, None] * (scaled_rows - middle_normalized_rows * (middle_inner_product / MODEL_WIDTH)[:, None])
    return (stream_mid_gradient.astype(jnp.bfloat16), d_w_down)
```

```python
import functools
import math

import jax
import jax.numpy as jnp
from jax import lax
from jax.experimental import pallas as pl
from jax.experimental.pallas import tpu as pltpu
from jax.sharding import PartitionSpec as P

EPSILON = 1e-05
MESH = pl.DeviceIdType.MESH
F32 = jnp.float32
BF16 = jnp.bfloat16


def nt(left, right):
    return lax.dot_general(left, right, (((1,), (1,)), ((), ())), preferred_element_type=F32)


def hint(value, factor):
    return pl.multiple_of(value, factor)


class Sems:
    def __init__(self, ref):
        self.ref, self.used = ref, 0

    def __call__(self):
        self.used += 1
        return self.ref.at[self.used - 1]


N_SEND, N_RECV, N_LOCAL = 96, 96, 24


def kernel(
    block_hbm, mid_hbm, gate_hbm, up_hbm, final_gain, mlp_gain, value_weight, token_hbm, w_gate, w_up, w_down,
    out_hbm, hid, dout_hbm,
    blk, mid, gains, tok, gx, ux, wd, wg, wu, fa, fb, hid_own,
    square, stat, share, tile, head8, head_j, dout, part_sum,
    rf, nl, nr, ha, hb, ml, mr, my, dg, yf, yb, sb, zs, zr, vs, dn, fin, outv,
    send_sems, recv_sems, local_sems, z_sems,
):
    t, width = blk.shape
    half = gx.shape[2]
    feat = width // 2
    tokens = 16 * t
    model = 8 * width
    n_tile = min(256, half)
    f_tile = min(256, feat)
    r, c = lax.axis_index("row"), lax.axis_index("col")
    k, j = lax.rem(r, 2), lax.div(r, 2)
    x, y = lax.div(j, 2), lax.rem(j, 2)
    z, b = lax.div(c, 2), lax.rem(c, 2)
    k1, y1, b1 = 1 - k, 1 - y, 1 - b
    xr, xl, xf = lax.rem(x + 1, 4), lax.rem(x + 3, 4), lax.rem(x + 2, 4)
    zp, zm, zf = lax.rem(z + 1, 4), lax.rem(z + 3, 4), lax.rem(z + 2, 4)
    sibling = (2 * j + k1, c)
    right, left = (4 * xr + 2 * y + k, c), (4 * xl + 2 * y + k, c)
    partner = (4 * x + 2 * y1 + k, c)
    z_plus, z_minus = (r, 2 * zp + b), (r, 2 * zm + b)
    own_half = pl.ds(hint(k * half, 128), half)
    other_half = pl.ds(hint(k1 * half, 128), half)
    diagonal = j == c
    off_diagonal = j != c
    new_send, new_recv, new_local = Sems(send_sems), Sems(recv_sems), Sems(local_sems)
    sent = []

    def send(src, dst, to, recv, when=None):
        copy = pltpu.make_async_remote_copy(
            src_ref=src, dst_ref=dst, send_sem=new_send(), recv_sem=recv, device_id=to, device_id_type=MESH
        )
        if when is None:
            copy.start()
        else:
            pl.when(when)(copy.start)
        sent.append((copy, when))

    def arrived(dst, recv):
        pltpu.make_async_copy(dst, dst, recv).wait()

    def fetch(src, dst):
        copy = pltpu.make_async_copy(src, dst, new_local())
        copy.start()
        return copy

    barrier = pltpu.get_barrier_semaphore()

    def greet(device):
        pl.semaphore_signal(barrier, inc=1, device_id=device, device_id_type=MESH)

    def perm_to(which):
        return (2 * c + k, 2 * x + which)

    def perm_from(which):
        return (2 * (2 * z + which) + k, j)

    for step in range(1, 8):
        greet((r, lax.rem(c + step, 8)))
    for step in range(1, 16):
        greet((lax.rem(r + step, 16), c))
    greet(perm_to(y1))
    greet(perm_from(b1))

    @pl.when(off_diagonal)
    def _():
        greet(perm_to(y))
        greet(perm_from(b))

    small = [
        fetch(block_hbm, blk),
        fetch(mid_hbm, mid),
        fetch(final_gain, gains.at[0]),
        fetch(value_weight, gains.at[1]),
        fetch(mlp_gain, gains.at[2]),
        fetch(token_hbm, tok),
    ]
    halves = [fetch(gate_hbm.at[:, own_half], gx.at[k]), fetch(up_hbm.at[:, own_half], ux.at[k])]
    own_rows = pl.ds(hint(k * feat, 16), feat)
    weights_down = fetch(w_down.at[own_half, :], wd.at[k])
    weights_in = [fetch(w_gate.at[:, own_half], wg.at[own_rows]), fetch(w_up.at[:, own_half], wu.at[own_rows])]
    for copy in small:
        copy.wait()

    lane = lax.broadcasted_iota(jnp.int32, (t, 128), 1)
    head8[...] = jnp.broadcast_to(gains[0] * gains[1], head8.shape)
    block_wide = blk[...].astype(F32)
    mid_wide = mid[...].astype(F32)
    square[...] = jnp.zeros_like(square)
    sum_out = jnp.sum(block_wide * block_wide, axis=1, keepdims=True)
    sum_head = jnp.sum(block_wide * head8[0:1, :], axis=1, keepdims=True)
    sum_mid = jnp.sum(mid_wide * mid_wide, axis=1, keepdims=True)
    square[0:t, :] = jnp.where(
        lane == 0, sum_out, jnp.where(lane == 1, sum_head, jnp.where(lane == 2, sum_mid, 0.0))
    )
    stat[c] = jnp.transpose(square[...])[0:8, :]

    @pl.when(off_diagonal)
    def _():
        pl.semaphore_wait(barrier, 26)

    @pl.when(diagonal)
    def _():
        pl.semaphore_wait(barrier, 24)

    perm_same, perm_other, perm_head = new_recv(), new_recv(), new_recv()
    send(block_hbm, tile.at[k, j], perm_to(y), perm_same, off_diagonal)
    send(block_hbm, tile.at[k, j], perm_to(y1), perm_other)
    send(head8, head_j, perm_to(y), perm_head, off_diagonal)

    @pl.when(diagonal)
    def _():
        tile[k, j] = blk[...]
        head_j[...] = head8[...]

    stat_recv = []
    for step in range(1, 8):
        stat_recv.append(new_recv())
        send(stat.at[c], stat.at[c], (r, lax.rem(c + step, 8)), stat_recv[-1])
    gate_recv, up_recv, wd_recv, wg_recv, wu_recv = (new_recv() for _ in range(5))
    send(gate_hbm.at[:, other_half], gx.at[k], sibling, gate_recv)
    send(up_hbm.at[:, other_half], ux.at[k], sibling, up_recv)
    send(w_down.at[other_half, :], wd.at[k], sibling, wd_recv)

    for copy in halves:
        copy.wait()
    arrived(gx.at[k1], gate_recv)
    arrived(ux.at[k1], up_recv)
    for q in range(2):

        @pl.loop(0, t // 16)
        def _(i):
            rows = pl.ds(hint(i * 16, 16), 16)
            out_rows = pl.ds(hint(q * t + i * 16, 16), 16)
            gate, up = gx[q, rows, :].astype(F32), ux[q, rows, :].astype(F32)
            sig = jax.nn.sigmoid(gate)
            silu = gate * sig
            fa[out_rows, :] = up * sig * (1.0 + gate * (1.0 - sig))
            fb[out_rows, :] = silu
            hid_own[out_rows, :] = (silu * up).astype(BF16)

    for step in range(1, 8):
        arrived(stat.at[lax.rem(c + 8 - step, 8)], stat_recv[step - 1])
    total = stat[0]
    for i in range(1, 8):
        total = total + stat[i]
    inverse_out = lax.rsqrt(total[0:1] / model + EPSILON)
    inverse_mid = lax.rsqrt(total[2:3] / model + EPSILON)
    value = inverse_out * total[1:2]
    live = tok[1:2, :]
    miss = live * (value - tok[0:1, :])
    slope = inverse_out * miss
    row = lax.broadcasted_iota(jnp.int32, (8, 128), 0)
    own_share = pl.ds(hint(8 * r, 8), 8)
    share[own_share, :] = jnp.where(
        row == 0,
        slope,
        jnp.where(
            row == 1,
            -slope * inverse_out * value / model,
            jnp.where(row == 2, live, jnp.where(row == 3, inverse_mid, 0.0)),
        ),
    )
    share_recv = []
    for step in range(1, 16):
        share_recv.append(new_recv())
        send(share.at[own_share], share.at[own_share], (lax.rem(r + step, 16), c), share_recv[-1])

    def hid_slot(slot, rows=None):
        return hid.at[slot, :, own_half] if rows is None else hid.at[slot, pl.ds(rows, t), own_half]

    def hid_sib(slot):
        return hid.at[slot, :, other_half]

    hid_recv = [new_recv() for _ in range(8)]
    hid_sib_recv = [new_recv() for _ in range(8)]
    slot_own, slot_part = 2 * x + y, 2 * x + y1
    slot_l, slot_r, slot_f = 2 * xl + y, 2 * xr + y, 2 * xf + y
    slot_lo, slot_ro, slot_fo = 2 * xl + y1, 2 * xr + y1, 2 * xf + y1

    def pair(zz):
        return tile.at[k, pl.ds(2 * zz, 2)]

    def pair_sib(zz):
        return tile.at[k1, pl.ds(2 * zz, 2)]

    z_left, z_right, z_far_a, z_far_b = (new_recv() for _ in range(4))
    sib_tile = [new_recv() for _ in range(4)]

    @pl.when(off_diagonal)
    def _():
        arrived(tile.at[k, c], perm_same)
        arrived(head_j, perm_head)

    arrived(tile.at[k, 2 * z + b1], perm_other)
    send(pair(z), pair(z), z_plus, z_left)
    send(pair(z), pair(z), z_minus, z_right)
    send(pair(z), pair(z), sibling, sib_tile[0])

    own_hid = fetch(hid_own, hid_slot(slot_own))
    send(hid_own, hid_slot(slot_own), partner, hid_recv[0])
    send(hid_own, hid_slot(slot_own), right, hid_recv[1])
    send(hid_own, hid_slot(slot_own), left, hid_recv[2])
    send(hid_own, hid_slot(slot_own), sibling, hid_sib_recv[0])

    arrived(pair(zm), z_left)
    send(tile.at[k, 2 * zm], tile.at[k, 2 * zm], z_plus, z_far_a)
    send(pair(zm), pair(zm), sibling, sib_tile[1])
    arrived(pair(zp), z_right)
    send(tile.at[k, 2 * zp + 1], tile.at[k, 2 * zp + 1], z_minus, z_far_b)
    send(pair(zp), pair(zp), sibling, sib_tile[2])

    for step in range(1, 16):
        from_row = lax.rem(r + 16 - step, 16)
        arrived(share.at[pl.ds(hint(8 * from_row, 8), 8)], share_recv[step - 1])
    shares = share[...]
    which = lax.rem(lax.broadcasted_iota(jnp.int32, (128, 128), 0), 8)
    count = jnp.sum(jnp.sum(jnp.where(which == 2, shares, 0.0), axis=0, keepdims=True), axis=1, keepdims=True)
    factor = tokens * math.sqrt(model) / count
    columns = jnp.transpose(shares) * factor
    square[0:8, :] = share[own_share, :]
    own_columns = jnp.transpose(square[...])

    arrived(tile.at[k, 2 * zf], z_far_a)
    arrived(tile.at[k, 2 * zf + 1], z_far_b)
    send(pair(zf), pair(zf), sibling, sib_tile[3])
    for where, sem in zip((z, zm, zp, zf), sib_tile):
        arrived(pair_sib(where), sem)

    head_row = head_j[0:1, :]
    for s in range(8):
        for q in range(2):
            at = 8 * (2 * s + q)
            dout[(2 * s + q) * t : (2 * s + q + 1) * t, :] = (
                columns[0:t, at : at + 1] * head_row + columns[0:t, at + 1 : at + 2] * tile[q, s].astype(F32)
            ).astype(BF16)
    dout_copy = fetch(dout.at[:, pl.ds(hint(k * feat, 128), feat)], dout_hbm)
    own_dout = (
        (own_columns[0:t, 0:1] * factor) * head8[0:1, :] + (own_columns[0:t, 1:2] * factor) * blk[...].astype(F32)
    ).astype(BF16)
    outv[...] = own_dout
    inverse_mid_column = own_columns[0:t, 3:4]

    weights_down.wait()
    arrived(wd.at[k1], wd_recv)
    send(w_gate.at[:, other_half], wg.at[own_rows], sibling, wg_recv)
    send(w_up.at[:, other_half], wu.at[own_rows], sibling, wu_recv)

    def chunk(slot, first=0, size=2 * t):
        return part_sum.at[pl.ds(hint(slot * 2 * t + first, 16), size)]

    def hidden_pair(xs):
        rows = pl.ds(hint(xs * 4 * t, 16), 4 * t)

        @pl.loop(0, half // n_tile)
        def _(n):
            units = pl.ds(hint(n * n_tile, 128), n_tile)
            part_sum[rows, units] = (
                nt(dout[rows, 0:feat], wd[0, units, :]) + nt(dout[rows, feat:], wd[1, units, :])
            ).astype(BF16)

    def add_into(slot, other, first=0, size=2 * t):
        @pl.loop(0, size // 16)
        def _(i):
            rows = pl.ds(hint(slot * 2 * t + first + i * 16, 16), 16)
            their = pl.ds(hint(i * 16, 16), 16)
            part_sum[rows, :] = (part_sum[rows, :].astype(F32) + other[their, :].astype(F32)).astype(BF16)

    rf_s, nl_s, nr_s, ha_s, hb_s, ml_s, mr_s, my_s = (new_recv() for _ in range(8))
    hidden_pair(xf)
    send(chunk(slot_fo), rf, partner, rf_s)
    hidden_pair(xr)
    send(chunk(slot_ro), nl, right, nl_s)
    hidden_pair(xl)
    send(chunk(slot_lo), nr, left, nr_s)
    hidden_pair(x)
    arrived(rf, rf_s)
    add_into(slot_f, rf)
    send(chunk(slot_f, 0, t), ha, right, ha_s)
    send(chunk(slot_f, t, t), hb, left, hb_s)
    arrived(nl, nl_s)
    add_into(slot_part, nl)
    arrived(nr, nr_s)
    add_into(slot_part, nr)
    send(chunk(slot_part), my, partner, my_s)
    arrived(ha, ha_s)
    add_into(slot_r, ha, 0, t)
    send(chunk(slot_r), ml, right, ml_s)
    arrived(hb, hb_s)
    add_into(slot_l, hb, t, t)
    send(chunk(slot_l), mr, left, mr_s)
    arrived(my, my_s)
    arrived(ml, ml_s)
    arrived(mr, mr_s)

    @pl.loop(0, 2 * t // 16)
    def _(i):
        rows = pl.ds(hint(i * 16, 16), 16)
        d_hidden = (
            part_sum[pl.ds(hint(slot_own * 2 * t + i * 16, 16), 16), :].astype(F32)
            + ml[rows, :].astype(F32)
            + mr[rows, :].astype(F32)
            + my[rows, :].astype(F32)
        )
        dg[slot_own, 0, rows, :] = (d_hidden * fa[rows, :]).astype(BF16)
        dg[slot_own, 1, rows, :] = (d_hidden * fb[rows, :]).astype(BF16)

    dg_recv = [new_recv() for _ in range(8)]
    sb_recv = [new_recv() for _ in range(8)]
    pending = []
    last = []

    def product(slot):
        @pl.loop(0, width // f_tile)
        def _(n):
            features = pl.ds(hint(n * f_tile, 128), f_tile)
            piece = nt(dg[slot, 0], wg[features, :]) + nt(dg[slot, 1], wu[features, :])
            yf[slot, :, features] = piece
            yb[slot, :, features] = piece.astype(BF16)

        sem = sb_recv[len(last) + len(pending)]
        send(yb.at[slot, pl.ds(hint(k1 * t, 16), t)], sb.at[slot], sibling, sem)
        pending.append((slot, sem))

    def combine():
        slot, sem = pending.pop(0)
        arrived(sb.at[slot], sem)
        zz, bb = lax.div(slot, 2), lax.rem(slot, 2)
        both = (yf[slot, pl.ds(hint(k * t, 16), t), :] + sb[slot].astype(F32)).astype(BF16)
        zs[slot] = both
        send(zs.at[slot], zr.at[bb, z], (r, 2 * zz + b), z_sems.at[bb, z], zz != z)

        @pl.when(zz == z)
        def _():
            zr[bb, z] = both

        last.append(slot)

    def whole(slot):
        return dg.at[slot]

    send(whole(slot_own), whole(slot_own), right, dg_recv[1])
    send(whole(slot_own), whole(slot_own), left, dg_recv[2])
    send(whole(slot_own), whole(slot_own), partner, dg_recv[0])
    for copy in weights_in:
        copy.wait()
    other_rows = pl.ds(hint(k1 * feat, 16), feat)
    arrived(wg.at[other_rows], wg_recv)
    arrived(wu.at[other_rows], wu_recv)
    product(slot_own)
    arrived(whole(slot_l), dg_recv[1])
    send(dg.at[slot_l, 0], dg.at[slot_l, 0], right, dg_recv[3])
    arrived(whole(slot_r), dg_recv[2])
    send(dg.at[slot_r, 1], dg.at[slot_r, 1], left, dg_recv[4])
    arrived(whole(slot_part), dg_recv[0])
    send(whole(slot_part), whole(slot_part), right, dg_recv[5])
    send(whole(slot_part), whole(slot_part), left, dg_recv[6])
    combine()
    product(slot_l)
    product(slot_r)
    combine()
    combine()
    product(slot_part)
    combine()
    arrived(dg.at[slot_f, 0], dg_recv[3])
    arrived(dg.at[slot_f, 1], dg_recv[4])
    send(whole(slot_f), whole(slot_f), partner, dg_recv[7])

    arrived(hid_slot(slot_l), hid_recv[1])
    send(hid_slot(slot_l, 0), hid_slot(slot_l, 0), right, hid_recv[3])
    arrived(hid_slot(slot_r), hid_recv[2])
    send(hid_slot(slot_r, t), hid_slot(slot_r, t), left, hid_recv[4])
    arrived(hid_slot(slot_part), hid_recv[0])
    send(hid_slot(slot_part), hid_slot(slot_part), right, hid_recv[5])
    send(hid_slot(slot_part), hid_slot(slot_part), left, hid_recv[6])
    send(hid_slot(slot_l), hid_slot(slot_l), sibling, hid_sib_recv[1])
    send(hid_slot(slot_r), hid_slot(slot_r), sibling, hid_sib_recv[2])
    send(hid_slot(slot_part), hid_slot(slot_part), sibling, hid_sib_recv[3])

    product(slot_f)
    combine()
    arrived(whole(slot_lo), dg_recv[5])
    product(slot_lo)
    arrived(whole(slot_ro), dg_recv[6])
    product(slot_ro)
    combine()
    combine()
    arrived(whole(slot_fo), dg_recv[7])
    product(slot_fo)
    combine()

    for q in range(2):
        for step in range(1, 4):
            zz = lax.rem(z + step, 4)
            arrived(zr.at[q, zz], z_sems.at[q, zz])

    def over_z(q):
        return zr[q, 0].astype(F32) + zr[q, 1].astype(F32) + zr[q, 2].astype(F32) + zr[q, 3].astype(F32)

    dn_same, dn_other = new_recv(), new_recv()
    vs[0] = over_z(0).astype(BF16)
    vs[1] = over_z(1).astype(BF16)
    send(vs.at[b1], dn.at[1], perm_from(b1), dn_other)
    send(vs.at[b], dn.at[0], perm_from(b), dn_same, off_diagonal)

    @pl.when(diagonal)
    def _():
        dn[0] = vs[b]

    arrived(hid_slot(slot_f, 0), hid_recv[3])
    arrived(hid_slot(slot_f, t), hid_recv[4])
    send(hid_slot(slot_f), hid_slot(slot_f), partner, hid_recv[7])
    send(hid_slot(slot_f), hid_slot(slot_f), sibling, hid_sib_recv[4])

    @pl.when(off_diagonal)
    def _():
        arrived(dn.at[0], dn_same)

    arrived(dn.at[1], dn_other)
    scaled = (dn[0].astype(F32) + dn[1].astype(F32)) * gains[2]
    normed = mid[...].astype(F32) * inverse_mid_column
    inner = jnp.sum(scaled * normed, axis=1, keepdims=True)
    square[0:t, :] = jnp.broadcast_to(inner, (t, 128))
    fin[c] = jnp.transpose(square[...])[0:8, :]
    fin_recv = []
    for step in range(1, 8):
        fin_recv.append(new_recv())
        send(fin.at[c], fin.at[c], (r, lax.rem(c + step, 8)), fin_recv[-1])

    arrived(hid_slot(slot_lo), hid_recv[5])
    send(hid_slot(slot_lo), hid_slot(slot_lo), sibling, hid_sib_recv[5])
    arrived(hid_slot(slot_ro), hid_recv[6])
    send(hid_slot(slot_ro), hid_slot(slot_ro), sibling, hid_sib_recv[6])
    arrived(hid_slot(slot_fo), hid_recv[7])
    send(hid_slot(slot_fo), hid_slot(slot_fo), sibling, hid_sib_recv[7])

    for step in range(1, 8):
        arrived(fin.at[lax.rem(c + 8 - step, 8)], fin_recv[step - 1])
    total = fin[0]
    for i in range(1, 8):
        total = total + fin[i]
    square[0:8, :] = total
    inner_column = jnp.transpose(square[...])[0:t, 0:1]
    outv[...] = (
        outv[...].astype(F32) + inverse_mid_column * (scaled - normed * (inner_column / model))
    ).astype(BF16)
    final = fetch(outv, out_hbm)

    order = (slot_own, slot_l, slot_r, slot_part, slot_f, slot_lo, slot_ro, slot_fo)
    for slot, sem in zip(order, hid_sib_recv):
        arrived(hid_sib(slot), sem)
    own_hid.wait()
    dout_copy.wait()
    final.wait()
    for copy, when in sent:
        if when is None:
            copy.wait_send()
        else:
            pl.when(when)(copy.wait_send)


def local(
    block_out, stream_mid, gate_pre, up_pre, final_gain, mlp_gain, value_weight, returns, response_mask, w_gate, w_up, w_down
):
    t, width = block_out.shape
    units = gate_pre.shape[1]
    half, feat = units // 2, width // 2
    token_rows = jnp.pad(
        jnp.stack([returns, response_mask.astype(F32)]), ((0, 6), (0, 128 - t))
    )
    any_spec = pl.BlockSpec(memory_space=pl.ANY)
    vm = pltpu.VMEM
    out, hid, dout = pl.pallas_call(
        kernel,
        out_shape=(
            jax.ShapeDtypeStruct((t, width), BF16),
            jax.ShapeDtypeStruct((8, 2 * t, units), BF16),
            jax.ShapeDtypeStruct((16 * t, feat), BF16),
        ),
        in_specs=[any_spec] * 11,
        out_specs=(any_spec,) * 3,
        scratch_shapes=[
            vm((t, width), BF16),
            vm((t, width), BF16),
            vm((3, 1, width), F32),
            vm((8, 128), F32),
            vm((2, t, half), BF16),
            vm((2, t, half), BF16),
            vm((2, half, feat), BF16),
            vm((width, half), BF16),
            vm((width, half), BF16),
            vm((2 * t, half), F32),
            vm((2 * t, half), F32),
            vm((2 * t, half), BF16),
            vm((128, 128), F32),
            vm((8, 8, 128), F32),
            vm((128, 128), F32),
            vm((2, 8, t, width), BF16),
            vm((8, width), F32),
            vm((8, width), F32),
            vm((16 * t, width), BF16),
            vm((16 * t, half), BF16),
            vm((2 * t, half), BF16),
            vm((2 * t, half), BF16),
            vm((2 * t, half), BF16),
            vm((t, half), BF16),
            vm((t, half), BF16),
            vm((2 * t, half), BF16),
            vm((2 * t, half), BF16),
            vm((2 * t, half), BF16),
            vm((8, 2, 2 * t, half), BF16),
            vm((8, 2 * t, width), F32),
            vm((8, 2 * t, width), BF16),
            vm((8, t, width), BF16),
            vm((8, t, width), BF16),
            vm((2, 4, t, width), BF16),
            vm((2, t, width), BF16),
            vm((2, t, width), BF16),
            vm((8, 8, 128), F32),
            vm((t, width), BF16),
            pltpu.SemaphoreType.DMA((N_SEND,)),
            pltpu.SemaphoreType.DMA((N_RECV,)),
            pltpu.SemaphoreType.DMA((N_LOCAL,)),
            pltpu.SemaphoreType.DMA((2, 4)),
        ],
        compiler_params=pltpu.CompilerParams(
            collective_id=0, has_side_effects=True, vmem_limit_bytes=60 * 1024 * 1024
        ),
    )(
        block_out, stream_mid, gate_pre, up_pre,
        final_gain.reshape(1, width), mlp_gain.reshape(1, width), value_weight.reshape(1, width),
        token_rows, w_gate, w_up, w_down,
    )
    d_w_down = lax.dot_general(
        hid.reshape(16 * t, units), dout, (((0,), (0,)), ((), ())), preferred_element_type=F32
    )
    return out, d_w_down


def solution(mesh):
    placed = (
        P("row", "col"), P("row", "col"), P("row", "col"), P("row", "col"),
        P("col"), P("col"), P("col"), P("row"), P("row"),
        P("row", "col"), P("row", "col"), P("col", "row"),
    )
    return jax.shard_map(
        local, mesh=mesh, in_specs=placed, out_specs=(P("row", "col"), P("col", "row")), check_vma=False
    )
```

```python
import functools
import math

import jax
import jax.numpy as jnp
from jax import lax
from jax.experimental import pallas as pl
from jax.experimental.pallas import tpu as pltpu
from jax.sharding import PartitionSpec as P

EPSILON = 1e-05
MESH = pl.DeviceIdType.MESH
F32 = jnp.float32
BF16 = jnp.bfloat16


def dot(left, right):
    return lax.dot_general(left, right, (((1,), (0,)), ((), ())), preferred_element_type=F32)


def hint(value, factor):
    return pl.multiple_of(value, factor)


class Sems:
    def __init__(self, ref):
        self.ref, self.used = ref, 0

    def __call__(self):
        self.used += 1
        return self.ref.at[self.used - 1]


N_SEND, N_RECV, N_LOCAL = 160, 160, 24


def kernel(
    block_hbm, mid_hbm, gate_hbm, up_hbm, final_gain, mlp_gain, value_weight, returns, mask, w_gate, w_up, w_down,
    out_hbm, hid, dout_hbm,
    blk, mid, gains, ret, msk, pack, gx, ux, wd, wg, wu, wdt, wgt, wut, fa, fb, hid_own,
    square, stat, share, tile, head, head_j, dout, part_sum,
    rf, nl, nr, ha, hb, ml, mr, my, dg, yf, yb, sb, zs, zr, vs, dn, fin, outv,
    send_sems, recv_sems, local_sems, z_sems, d_sems,
):
    t, width = blk.shape
    half = gx.shape[2]
    feat = width // 2
    tokens = 16 * t
    model = 8 * width
    first = (half // 2 + 255) // 256 * 256 if half >= 512 else half // 2
    pieces = (pl.ds(0, first), pl.ds(first, half - first))
    r, c = lax.axis_index("row"), lax.axis_index("col")
    k, j = lax.rem(r, 2), lax.div(r, 2)
    x, y = lax.div(j, 2), lax.rem(j, 2)
    z, b = lax.div(c, 2), lax.rem(c, 2)
    k1, y1, b1 = 1 - k, 1 - y, 1 - b
    xr, xl, xf = lax.rem(x + 1, 4), lax.rem(x + 3, 4), lax.rem(x + 2, 4)
    zp, zm, zf = lax.rem(z + 1, 4), lax.rem(z + 3, 4), lax.rem(z + 2, 4)
    sibling = (2 * j + k1, c)
    right, left = (4 * xr + 2 * y + k, c), (4 * xl + 2 * y + k, c)
    partner = (4 * x + 2 * y1 + k, c)
    z_plus, z_minus, z_partner = (r, 2 * zp + b), (r, 2 * zm + b), (r, 2 * z + b1)
    slot_own, slot_part = 2 * x + y, 2 * x + y1
    slot_l, slot_r, slot_f = 2 * xl + y, 2 * xr + y, 2 * xf + y
    slot_lo, slot_ro, slot_fo = 2 * xl + y1, 2 * xr + y1, 2 * xf + y1
    own_half = pl.ds(hint(k * half, 128), half)
    other_half = pl.ds(hint(k1 * half, 128), half)
    diagonal = j == c
    off_diagonal = j != c
    new_send, new_recv, new_local = Sems(send_sems), Sems(recv_sems), Sems(local_sems)
    sent = []

    def send(src, dst, to, recv, when=None):
        copy = pltpu.make_async_remote_copy(
            src_ref=src, dst_ref=dst, send_sem=new_send(), recv_sem=recv, device_id=to, device_id_type=MESH
        )
        if when is None:
            copy.start()
        else:
            pl.when(when)(copy.start)
        sent.append((copy, when))

    def send_same(ref, to, recv):
        send(ref, ref, to, recv)

    def arrived(dst, recv):
        pltpu.make_async_copy(dst, dst, recv).wait()

    def fetch(src, dst):
        copy = pltpu.make_async_copy(src, dst, new_local())
        copy.start()
        return copy

    barrier = pltpu.get_barrier_semaphore()

    def greet(device):
        pl.semaphore_signal(barrier, inc=1, device_id=device, device_id_type=MESH)

    def perm_to(which):
        return (2 * c + k, 2 * x + which)

    def perm_from(which):
        return (2 * (2 * z + which) + k, j)

    greet(perm_to(y1))
    greet(perm_from(b1))

    @pl.when(off_diagonal)
    def _():
        greet(perm_to(y))
        greet(perm_from(b))

    for step in (4, 5, 3, 6, 2, 7, 1):
        greet((r, lax.rem(c + step, 8)))
    for step in (8, 9, 7, 10, 6, 11, 5, 12, 4, 13, 3, 14, 2, 15, 1):
        greet((lax.rem(r + step, 16), c))

    small = [
        fetch(block_hbm, blk),
        fetch(mid_hbm, mid),
        fetch(final_gain, gains.at[0]),
        fetch(value_weight, gains.at[1]),
        fetch(mlp_gain, gains.at[2]),
        fetch(returns, ret),
        fetch(mask, msk),
    ]
    halves = [fetch(gate_hbm.at[:, own_half], gx.at[k]), fetch(up_hbm.at[:, own_half], ux.at[k])]
    own_rows = pl.ds(hint(k * feat, 16), feat)
    weights_down = fetch(w_down.at[own_half, :], wd.at[k])
    weights_in = [fetch(w_gate.at[:, own_half], wg.at[own_rows]), fetch(w_up.at[:, own_half], wu.at[own_rows])]
    for copy in small:
        copy.wait()

    lane = lax.broadcasted_iota(jnp.int32, (t, 128), 1)
    head[...] = gains[0] * gains[1]
    block_wide = blk[...].astype(F32)
    mid_wide = mid[...].astype(F32)
    square[...] = jnp.zeros_like(square)
    pack[...] = jnp.zeros_like(pack)
    sum_out = jnp.sum(block_wide * block_wide, axis=1, keepdims=True)
    sum_head = jnp.sum(block_wide * head[...], axis=1, keepdims=True)
    sum_mid = jnp.sum(mid_wide * mid_wide, axis=1, keepdims=True)
    square[0:t, :] = jnp.where(
        lane == 0, sum_out, jnp.where(lane == 1, sum_head, jnp.where(lane == 2, sum_mid, 0.0))
    )
    stat[c] = jnp.transpose(square[...])[0:8, :]

    @pl.when(off_diagonal)
    def _():
        pl.semaphore_wait(barrier, 26)

    @pl.when(diagonal)
    def _():
        pl.semaphore_wait(barrier, 24)

    stat_recv = {}
    for step in (4, 5, 3, 6, 2, 7, 1):
        stat_recv[step] = new_recv()
        send_same(stat.at[c], (r, lax.rem(c + step, 8)), stat_recv[step])
    perm_recv, perm_head = new_recv(), new_recv()
    send(block_hbm, tile.at[k, j], perm_to(y), perm_recv, off_diagonal)
    send(head, head_j, perm_to(y), perm_head, off_diagonal)

    @pl.when(diagonal)
    def _():
        tile[k, j] = blk[...]
        head_j[...] = head[...]

    gate_recv, up_recv, wd_recv, wg_recv, wu_recv = (new_recv() for _ in range(5))
    send(gate_hbm.at[:, other_half], gx.at[k], sibling, gate_recv)
    send(up_hbm.at[:, other_half], ux.at[k], sibling, up_recv)
    send(w_down.at[other_half, :], wd.at[k], sibling, wd_recv)

    for copy in halves:
        copy.wait()
    arrived(gx.at[k1], gate_recv)
    arrived(ux.at[k1], up_recv)
    for q in range(2):

        @pl.loop(0, t // 16)
        def _(i):
            rows = pl.ds(hint(i * 16, 16), 16)
            out_rows = pl.ds(hint(q * t + i * 16, 16), 16)
            gate, up = gx[q, rows, :].astype(F32), ux[q, rows, :].astype(F32)
            sig = jax.nn.sigmoid(gate)
            silu = gate * sig
            fa[out_rows, :] = up * sig * (1.0 + gate * (1.0 - sig))
            fb[out_rows, :] = silu
            hid_own[out_rows, :] = (silu * up).astype(BF16)

    def hid_slot(slot, rows=None):
        return hid.at[slot, :, own_half] if rows is None else hid.at[slot, pl.ds(rows, t), own_half]

    hid_recv = [new_recv() for _ in range(8)]
    hid_sib = []

    def hid_to_sibling(slot):
        hid_sib.append((slot, new_recv()))
        send_same(hid_slot(slot), sibling, hid_sib[-1][1])

    own_hid = fetch(hid_own, hid_slot(slot_own))
    send(hid_own, hid_slot(slot_own), partner, hid_recv[0])
    send(hid_own, hid_slot(slot_own), right, hid_recv[1])
    send(hid_own, hid_slot(slot_own), left, hid_recv[2])

    for step in (1, 7, 2, 6, 3, 5, 4):
        arrived(stat.at[lax.rem(c + 8 - step, 8)], stat_recv[step])
    total = stat[0]
    for i in range(1, 8):
        total = total + stat[i]
    total = total[:, 0:t]
    inverse_out = lax.rsqrt(total[0:1] / model + EPSILON)
    value = inverse_out * total[1:2]
    live = msk[...].astype(F32)
    slope = inverse_out * (live * (value - ret[...]))
    pack[0:1, 0:t] = slope
    pack[1:2, 0:t] = -slope * inverse_out * value / model
    pack[2:3, 0:t] = live
    pack[3:4, 0:t] = lax.rsqrt(total[2:3] / model + EPSILON)
    own_share = pl.ds(hint(8 * r, 8), 8)
    share[own_share, :] = pack[...]
    share_recv = {}
    for step in (8, 9, 7, 10, 6, 11, 5, 12, 4, 13, 3, 14, 2, 15, 1):
        share_recv[step] = new_recv()
        send_same(share.at[own_share], (lax.rem(r + step, 16), c), share_recv[step])

    sib_tile = []

    def tile_to_sibling(slot):
        sib_tile.append((slot, new_recv()))
        send_same(tile.at[k, slot], sibling, sib_tile[-1][1])

    t_part, t_own_m, t_own_p, t_oth_m, t_oth_p, t_far_own, t_far_oth = (new_recv() for _ in range(7))

    @pl.when(off_diagonal)
    def _():
        arrived(tile.at[k, c], perm_recv)
        arrived(head_j, perm_head)

    send_same(tile.at[k, c], z_partner, t_part)
    send_same(tile.at[k, c], z_plus, t_own_m)
    send_same(tile.at[k, c], z_minus, t_own_p)
    tile_to_sibling(c)

    weights_down.wait()
    arrived(wd.at[k1], wd_recv)
    u_tile = 256 if half % 256 == 0 else 128
    for q in range(2):

        @pl.loop(0, half // u_tile)
        def _(n):
            units = pl.ds(hint(n * u_tile, 128), u_tile)
            wdt[q * feat : (q + 1) * feat, units] = jnp.transpose(wd[q, units, :])

    arrived(tile.at[k, 2 * zm + b], t_own_m)
    send_same(tile.at[k, 2 * zm + b], z_plus, t_far_own)
    tile_to_sibling(2 * zm + b)
    arrived(tile.at[k, 2 * z + b1], t_part)
    send_same(tile.at[k, 2 * z + b1], z_plus, t_oth_m)
    send_same(tile.at[k, 2 * z + b1], z_minus, t_oth_p)
    tile_to_sibling(2 * z + b1)
    arrived(tile.at[k, 2 * zp + b], t_own_p)
    tile_to_sibling(2 * zp + b)

    arrived(hid_slot(slot_l), hid_recv[1])
    send_same(hid_slot(slot_l, 0), right, hid_recv[3])
    arrived(hid_slot(slot_r), hid_recv[2])
    send_same(hid_slot(slot_r, t), left, hid_recv[4])
    arrived(hid_slot(slot_part), hid_recv[0])
    send_same(hid_slot(slot_part), right, hid_recv[5])
    send_same(hid_slot(slot_part), left, hid_recv[6])

    arrived(tile.at[k, 2 * zp + b1], t_oth_p)
    send_same(tile.at[k, 2 * zp + b1], z_minus, t_far_oth)
    tile_to_sibling(2 * zp + b1)
    arrived(tile.at[k, 2 * zm + b1], t_oth_m)
    tile_to_sibling(2 * zm + b1)
    arrived(tile.at[k, 2 * zf + b], t_far_own)
    tile_to_sibling(2 * zf + b)

    for step in (1, 15, 2, 14, 3, 13, 4, 12, 5, 11, 6, 10, 7, 9, 8):
        from_row = lax.rem(r + 16 - step, 16)
        arrived(share.at[pl.ds(hint(8 * from_row, 8), 8)], share_recv[step])
    shares = share[...]
    which = lax.rem(lax.broadcasted_iota(jnp.int32, (128, 128), 0), 8)
    count = jnp.sum(jnp.sum(jnp.where(which == 2, shares, 0.0), axis=0, keepdims=True), axis=1, keepdims=True)
    factor = tokens * math.sqrt(model) / count
    columns = jnp.transpose(shares) * factor
    square[0:8, :] = pack[...]
    own_columns = jnp.transpose(square[...])

    arrived(tile.at[k, 2 * zf + b1], t_far_oth)
    tile_to_sibling(2 * zf + b1)
    send(w_gate.at[:, other_half], wg.at[own_rows], sibling, wg_recv)
    send(w_up.at[:, other_half], wu.at[own_rows], sibling, wu_recv)
    for slot, sem in sib_tile:
        arrived(tile.at[k1, slot], sem)

    head_row = head_j[...]
    for s in range(8):
        for q in range(2):
            at = 8 * (2 * s + q)
            dout[(2 * s + q) * t : (2 * s + q + 1) * t, :] = (
                columns[0:t, at : at + 1] * head_row + columns[0:t, at + 1 : at + 2] * tile[q, s].astype(F32)
            ).astype(BF16)
    dout_copy = fetch(dout.at[:, pl.ds(hint(k * feat, 128), feat)], dout_hbm)

    def chunk(slot, piece, start=0, size=2 * t):
        return part_sum.at[pl.ds(hint(slot * 2 * t + start, 16), size), piece]

    def hidden(slot, piece):
        rows = pl.ds(hint(slot * 2 * t, 16), 2 * t)
        part_sum[rows, piece] = dot(dout[rows, :], wdt[:, piece]).astype(BF16)

    def add_into(slot, piece, others, start=0, size=2 * t):
        @pl.loop(0, size // 16)
        def _(i):
            rows = pl.ds(hint(slot * 2 * t + start + i * 16, 16), 16)
            their = pl.ds(hint(i * 16, 16), 16)
            value = part_sum[rows, piece].astype(F32)
            for other in others:
                value = value + other[their, piece].astype(F32)
            part_sum[rows, piece] = value.astype(BF16)

    both = (0, 1)
    rf_s, nl_s, nr_s, ha_s, hb_s, ml_s, mr_s, my_s = ([new_recv(), new_recv()] for _ in range(8))
    for h in both:
        hidden(slot_fo, pieces[h])
        send(chunk(slot_fo, pieces[h]), rf.at[:, pieces[h]], partner, rf_s[h])
        hidden(slot_ro, pieces[h])
        send(chunk(slot_ro, pieces[h]), nl.at[:, pieces[h]], right, nl_s[h])
        hidden(slot_lo, pieces[h])
        send(chunk(slot_lo, pieces[h]), nr.at[:, pieces[h]], left, nr_s[h])
    for h in both:
        hidden(slot_f, pieces[h])
        arrived(rf.at[:, pieces[h]], rf_s[h])
        add_into(slot_f, pieces[h], (rf,))
        send(chunk(slot_f, pieces[h], 0, t), ha.at[:, pieces[h]], right, ha_s[h])
        send(chunk(slot_f, pieces[h], t, t), hb.at[:, pieces[h]], left, hb_s[h])
    for h in both:
        hidden(slot_part, pieces[h])
    for h in both:
        hidden(slot_r, pieces[h])
        hidden(slot_l, pieces[h])
        arrived(nl.at[:, pieces[h]], nl_s[h])
        arrived(nr.at[:, pieces[h]], nr_s[h])
        add_into(slot_part, pieces[h], (nl, nr))
        send(chunk(slot_part, pieces[h]), my.at[:, pieces[h]], partner, my_s[h])
    for h in both:
        arrived(ha.at[:, pieces[h]], ha_s[h])
        add_into(slot_r, pieces[h], (ha,), 0, t)
        send(chunk(slot_r, pieces[h]), ml.at[:, pieces[h]], right, ml_s[h])
        arrived(hb.at[:, pieces[h]], hb_s[h])
        add_into(slot_l, pieces[h], (hb,), t, t)
        send(chunk(slot_l, pieces[h]), mr.at[:, pieces[h]], left, mr_s[h])
    for h in both:
        hidden(slot_own, pieces[h])

    arrived(hid_slot(slot_f, 0), hid_recv[3])
    arrived(hid_slot(slot_f, t), hid_recv[4])
    send_same(hid_slot(slot_f), partner, hid_recv[7])
    own_hid.wait()
    for slot in (slot_own, slot_l, slot_r, slot_part, slot_f):
        hid_to_sibling(slot)
    for copy in weights_in:
        copy.wait()
    other_rows = pl.ds(hint(k1 * feat, 16), feat)
    f_tile = 256 if width % 256 == 0 else 128
    for source, target, sem in ((wg, wgt, wg_recv), (wu, wut, wu_recv)):
        arrived(source.at[other_rows], sem)

        @pl.loop(0, width // f_tile)
        def _(n):
            features = pl.ds(hint(n * f_tile, 128), f_tile)
            target[:, features] = jnp.transpose(source[features, :])

    inverse_mid_column = own_columns[0:t, 3:4]
    outv[...] = (
        (own_columns[0:t, 0:1] * factor) * head[...] + (own_columns[0:t, 1:2] * factor) * blk[...].astype(F32)
    ).astype(BF16)

    dg_recv = [[new_recv(), new_recv()] for _ in range(8)]
    sb_recv = [new_recv() for _ in range(8)]
    pending, last = [], []

    def whole(slot, piece):
        return dg.at[slot, :, :, piece]

    def one(slot, which, piece):
        return dg.at[slot, which, :, piece]

    for h in both:
        piece = pieces[h]
        arrived(my.at[:, piece], my_s[h])
        arrived(ml.at[:, piece], ml_s[h])
        arrived(mr.at[:, piece], mr_s[h])

        @pl.loop(0, 2 * t // 16)
        def _(i):
            rows = pl.ds(hint(i * 16, 16), 16)
            d_hidden = (
                part_sum[pl.ds(hint(slot_own * 2 * t + i * 16, 16), 16), piece].astype(F32)
                + ml[rows, piece].astype(F32)
                + mr[rows, piece].astype(F32)
                + my[rows, piece].astype(F32)
            )
            dg[slot_own, 0, rows, piece] = (d_hidden * fa[rows, piece]).astype(BF16)
            dg[slot_own, 1, rows, piece] = (d_hidden * fb[rows, piece]).astype(BF16)

        send_same(whole(slot_own, piece), right, dg_recv[1][h])
        send_same(whole(slot_own, piece), left, dg_recv[2][h])
        send_same(whole(slot_own, piece), partner, dg_recv[0][h])

    def product(slot, h):
        piece = pieces[h]
        value = dot(dg[slot, 0, :, piece], wgt[piece, :]) + dot(dg[slot, 1, :, piece], wut[piece, :])
        if h == 0:
            yf[slot] = value
            return
        value = value + yf[slot]
        yf[slot] = value
        yb[slot] = value.astype(BF16)
        sem = sb_recv[len(last) + len(pending)]
        send(yb.at[slot, pl.ds(hint(k1 * t, 16), t)], sb.at[slot], sibling, sem)
        pending.append((slot, sem))

    def combine():
        slot, sem = pending.pop(0)
        arrived(sb.at[slot], sem)
        zz, bb = lax.div(slot, 2), lax.rem(slot, 2)
        summed = (yf[slot, pl.ds(hint(k * t, 16), t), :] + sb[slot].astype(F32)).astype(BF16)
        zs[slot] = summed
        send(zs.at[slot], zr.at[bb, z], (r, 2 * zz + b), z_sems.at[bb, z], zz != z)

        @pl.when(zz == z)
        def _():
            zr[bb, z] = summed

        last.append(slot)

    def over_z(q):
        for step in range(1, 4):
            zz = lax.rem(z + step, 4)
            arrived(zr.at[q, zz], z_sems.at[q, zz])
        vs[q] = (
            zr[q, 0].astype(F32) + zr[q, 1].astype(F32) + zr[q, 2].astype(F32) + zr[q, 3].astype(F32)
        ).astype(BF16)

    product(slot_own, 0)
    product(slot_own, 1)
    for h in both:
        arrived(whole(slot_l, pieces[h]), dg_recv[1][h])
        send_same(one(slot_l, 0, pieces[h]), right, dg_recv[3][h])
        arrived(whole(slot_r, pieces[h]), dg_recv[2][h])
        send_same(one(slot_r, 1, pieces[h]), left, dg_recv[4][h])
        if h == 0:
            combine()
            product(slot_l, 0)
            product(slot_r, 0)
    for h in both:
        arrived(whole(slot_part, pieces[h]), dg_recv[0][h])
        send_same(whole(slot_part, pieces[h]), right, dg_recv[5][h])
        send_same(whole(slot_part, pieces[h]), left, dg_recv[6][h])
    product(slot_l, 1)
    product(slot_r, 1)
    for h in both:
        arrived(one(slot_f, 0, pieces[h]), dg_recv[3][h])
        arrived(one(slot_f, 1, pieces[h]), dg_recv[4][h])
        send_same(whole(slot_f, pieces[h]), partner, dg_recv[7][h])
        if h == 0:
            combine()
            product(slot_part, 0)
            product(slot_part, 1)
            combine()
        product(slot_f, h)
    combine()
    combine()

    same = lax.rem(y + b, 2)
    over_z(y)
    send(vs.at[y], dn.at[same], perm_from(y), d_sems.at[same], off_diagonal)

    @pl.when(diagonal)
    def _():
        dn[same] = vs[y]

    arrived(hid_slot(slot_lo), hid_recv[5])
    hid_to_sibling(slot_lo)
    arrived(hid_slot(slot_ro), hid_recv[6])
    hid_to_sibling(slot_ro)
    arrived(hid_slot(slot_fo), hid_recv[7])
    hid_to_sibling(slot_fo)

    for h in both:
        arrived(whole(slot_fo, pieces[h]), dg_recv[7][h])
        product(slot_fo, h)
        arrived(whole(slot_lo, pieces[h]), dg_recv[5][h])
        product(slot_lo, h)
        arrived(whole(slot_ro, pieces[h]), dg_recv[6][h])
        product(slot_ro, h)
    combine()
    combine()
    combine()
    over_z(y1)
    send(vs.at[y1], dn.at[1 - same], perm_from(y1), d_sems.at[1 - same])

    for slot, sem in hid_sib:
        arrived(hid.at[slot, :, other_half], sem)

    @pl.when(off_diagonal)
    def _():
        arrived(dn.at[0], d_sems.at[0])

    arrived(dn.at[1], d_sems.at[1])
    scaled = (dn[0].astype(F32) + dn[1].astype(F32)) * gains[2]
    normed = mid[...].astype(F32) * inverse_mid_column
    inner = jnp.sum(scaled * normed, axis=1, keepdims=True)
    square[0:t, :] = jnp.broadcast_to(inner, (t, 128))
    fin[c] = jnp.transpose(square[...])[0:8, :]
    fin_recv = {}
    for step in (4, 5, 3, 6, 2, 7, 1):
        fin_recv[step] = new_recv()
        send_same(fin.at[c], (r, lax.rem(c + step, 8)), fin_recv[step])
    for step in (1, 7, 2, 6, 3, 5, 4):
        arrived(fin.at[lax.rem(c + 8 - step, 8)], fin_recv[step])
    total = fin[0]
    for i in range(1, 8):
        total = total + fin[i]
    square[0:8, :] = total
    inner_column = jnp.transpose(square[...])[0:t, 0:1]
    outv[...] = (
        outv[...].astype(F32) + inverse_mid_column * (scaled - normed * (inner_column / model))
    ).astype(BF16)
    final = fetch(outv, out_hbm)
    dout_copy.wait()
    final.wait()
    for copy, when in sent:
        if when is None:
            copy.wait_send()
        else:
            pl.when(when)(copy.wait_send)


def local(
    block_out, stream_mid, gate_pre, up_pre, final_gain, mlp_gain, value_weight, returns, response_mask, w_gate, w_up, w_down
):
    t, width = block_out.shape
    units = gate_pre.shape[1]
    half, feat = units // 2, width // 2
    any_spec = pl.BlockSpec(memory_space=pl.ANY)
    vm = pltpu.VMEM
    out, hid, dout = pl.pallas_call(
        kernel,
        out_shape=(
            jax.ShapeDtypeStruct((t, width), BF16),
            jax.ShapeDtypeStruct((8, 2 * t, units), BF16),
            jax.ShapeDtypeStruct((16 * t, feat), BF16),
        ),
        in_specs=[any_spec] * 12,
        out_specs=(any_spec,) * 3,
        scratch_shapes=[
            vm((t, width), BF16),
            vm((t, width), BF16),
            vm((3, 1, width), F32),
            vm((1, t), F32),
            vm((1, t), jnp.int32),
            vm((8, 128), F32),
            vm((2, t, half), BF16),
            vm((2, t, half), BF16),
            vm((2, half, feat), BF16),
            vm((width, half), BF16),
            vm((width, half), BF16),
            vm((width, half), BF16),
            vm((half, width), BF16),
            vm((half, width), BF16),
            vm((2 * t, half), F32),
            vm((2 * t, half), F32),
            vm((2 * t, half), BF16),
            vm((128, 128), F32),
            vm((8, 8, 128), F32),
            vm((128, 128), F32),
            vm((2, 8, t, width), BF16),
            vm((1, width), F32),
            vm((1, width), F32),
            vm((16 * t, width), BF16),
            vm((16 * t, half), BF16),
            vm((2 * t, half), BF16),
            vm((2 * t, half), BF16),
            vm((2 * t, half), BF16),
            vm((t, half), BF16),
            vm((t, half), BF16),
            vm((2 * t, half), BF16),
            vm((2 * t, half), BF16),
            vm((2 * t, half), BF16),
            vm((8, 2, 2 * t, half), BF16),
            vm((8, 2 * t, width), F32),
            vm((8, 2 * t, width), BF16),
            vm((8, t, width), BF16),
            vm((8, t, width), BF16),
            vm((2, 4, t, width), BF16),
            vm((2, t, width), BF16),
            vm((2, t, width), BF16),
            vm((8, 8, 128), F32),
            vm((t, width), BF16),
            pltpu.SemaphoreType.DMA((N_SEND,)),
            pltpu.SemaphoreType.DMA((N_RECV,)),
            pltpu.SemaphoreType.DMA((N_LOCAL,)),
            pltpu.SemaphoreType.DMA((2, 4)),
            pltpu.SemaphoreType.DMA((2,)),
        ],
        compiler_params=pltpu.CompilerParams(
            collective_id=0, has_side_effects=True, vmem_limit_bytes=60 * 1024 * 1024
        ),
    )(
        block_out, stream_mid, gate_pre, up_pre,
        final_gain.reshape(1, width), mlp_gain.reshape(1, width), value_weight.reshape(1, width),
        returns.reshape(1, t), response_mask.reshape(1, t), w_gate, w_up, w_down,
    )
    d_w_down = lax.dot_general(
        hid.reshape(16 * t, units), dout, (((0,), (0,)), ((), ())), preferred_element_type=F32
    )
    return out, d_w_down


def solution(mesh):
    placed = (
        P("row", "col"), P("row", "col"), P("row", "col"), P("row", "col"),
        P("col"), P("col"), P("col"), P("row"), P("row"),
        P("row", "col"), P("row", "col"), P("col", "row"),
    )
    return jax.shard_map(
        local, mesh=mesh, in_specs=placed, out_specs=(P("row", "col"), P("col", "row")), check_vma=False
    )
```

```python
import functools
import math

import jax
import jax.numpy as jnp
from jax import lax
from jax.experimental import pallas as pl
from jax.experimental.pallas import tpu as pltpu
from jax.sharding import PartitionSpec as P

EPSILON = 1e-05
MESH = pl.DeviceIdType.MESH
F32 = jnp.float32
BF16 = jnp.bfloat16


def dot(left, right):
    return lax.dot_general(left, right, (((1,), (0,)), ((), ())), preferred_element_type=F32)


def hint(value, factor):
    return pl.multiple_of(value, factor)


class Sems:
    def __init__(self, ref):
        self.ref, self.used = ref, 0

    def __call__(self):
        self.used += 1
        return self.ref.at[self.used - 1]


N_SEND, N_RECV, N_LOCAL = 160, 160, 24


def kernel(
    block_hbm, mid_hbm, gate_hbm, up_hbm, final_gain, mlp_gain, value_weight, returns, mask, w_gate, w_up, w_down,
    out_hbm, hid, dw_hbm,
    blk, mid, gains, ret, msk, pack, gx, ux, wd, wg, wu, wdt, wgt, wut, fa, fb, hid_own,
    square, stat, share, tile, head, head_j, dout, part_sum,
    rf, nl, nr, ha, hb, ml, mr, my, dg, yf, yb, sb, zs, zr, vs, dn, fin, outv,
    send_sems, recv_sems, local_sems, z_sems, d_sems,
):
    t, width = blk.shape
    half = gx.shape[2]
    feat = width // 2
    tokens = 16 * t
    model = 8 * width
    first = (half // 2 + 255) // 256 * 256 if half >= 512 else half // 2
    pieces = (pl.ds(0, first), pl.ds(first, half - first))
    r, c = lax.axis_index("row"), lax.axis_index("col")
    k, j = lax.rem(r, 2), lax.div(r, 2)
    x, y = lax.div(j, 2), lax.rem(j, 2)
    z, b = lax.div(c, 2), lax.rem(c, 2)
    k1, y1, b1 = 1 - k, 1 - y, 1 - b
    xr, xl, xf = lax.rem(x + 1, 4), lax.rem(x + 3, 4), lax.rem(x + 2, 4)
    zp, zm, zf = lax.rem(z + 1, 4), lax.rem(z + 3, 4), lax.rem(z + 2, 4)
    sibling = (2 * j + k1, c)
    right, left = (4 * xr + 2 * y + k, c), (4 * xl + 2 * y + k, c)
    partner = (4 * x + 2 * y1 + k, c)
    z_plus, z_minus, z_partner = (r, 2 * zp + b), (r, 2 * zm + b), (r, 2 * z + b1)
    slot_own, slot_part = 2 * x + y, 2 * x + y1
    slot_l, slot_r, slot_f = 2 * xl + y, 2 * xr + y, 2 * xf + y
    slot_lo, slot_ro, slot_fo = 2 * xl + y1, 2 * xr + y1, 2 * xf + y1
    own_half = pl.ds(hint(k * half, 128), half)
    other_half = pl.ds(hint(k1 * half, 128), half)
    diagonal = j == c
    off_diagonal = j != c
    new_send, new_recv, new_local = Sems(send_sems), Sems(recv_sems), Sems(local_sems)
    sent = []

    def send(src, dst, to, recv, when=None):
        copy = pltpu.make_async_remote_copy(
            src_ref=src, dst_ref=dst, send_sem=new_send(), recv_sem=recv, device_id=to, device_id_type=MESH
        )
        if when is None:
            copy.start()
        else:
            pl.when(when)(copy.start)
        sent.append((copy, when))

    def send_same(ref, to, recv):
        send(ref, ref, to, recv)

    def arrived(dst, recv):
        pltpu.make_async_copy(dst, dst, recv).wait()

    def fetch(src, dst):
        copy = pltpu.make_async_copy(src, dst, new_local())
        copy.start()
        return copy

    barrier = pltpu.get_barrier_semaphore()

    def greet(device):
        pl.semaphore_signal(barrier, inc=1, device_id=device, device_id_type=MESH)

    def perm_to(which):
        return (2 * c + k, 2 * x + which)

    def perm_from():
        return (2 * c + k, j)

    sum_x = lax.rem(z + 4 - x, 4)
    own_sum = jnp.logical_and(diagonal, x == 0)
    not_own_sum = jnp.logical_not(own_sum)

    def sum_to(which):
        return (2 * (2 * sum_x + which) + k, j)

    def sum_from(which):
        return (2 * c + k, 2 * lax.rem(x + z, 4) + which)

    greet(sum_to(b1))
    greet(sum_from(y1))

    @pl.when(not_own_sum)
    def _():
        greet(sum_to(b))
        greet(sum_from(y))

    @pl.when(off_diagonal)
    def _():
        greet(perm_to(y))
        greet(perm_from())

    for step in (4, 5, 3, 6, 2, 7, 1):
        greet((r, lax.rem(c + step, 8)))
    for step in (8, 9, 7, 10, 6, 11, 5, 12, 4, 13, 3, 14, 2, 15, 1):
        greet((lax.rem(r + step, 16), c))

    small = [
        fetch(block_hbm, blk),
        fetch(mid_hbm, mid),
        fetch(final_gain, gains.at[0]),
        fetch(value_weight, gains.at[1]),
        fetch(mlp_gain, gains.at[2]),
        fetch(returns, ret),
        fetch(mask, msk),
    ]
    halves = [fetch(gate_hbm.at[:, own_half], gx.at[k]), fetch(up_hbm.at[:, own_half], ux.at[k])]
    own_rows = pl.ds(hint(k * feat, 16), feat)
    weights_down = fetch(w_down.at[own_half, :], wd.at[k])
    weights_in = [fetch(w_gate.at[:, own_half], wg.at[own_rows]), fetch(w_up.at[:, own_half], wu.at[own_rows])]
    for copy in small:
        copy.wait()

    lane = lax.broadcasted_iota(jnp.int32, (t, 128), 1)
    head[...] = gains[0] * gains[1]
    block_wide = blk[...].astype(F32)
    mid_wide = mid[...].astype(F32)
    square[...] = jnp.zeros_like(square)
    pack[...] = jnp.zeros_like(pack)
    sum_out = jnp.sum(block_wide * block_wide, axis=1, keepdims=True)
    sum_head = jnp.sum(block_wide * head[...], axis=1, keepdims=True)
    sum_mid = jnp.sum(mid_wide * mid_wide, axis=1, keepdims=True)
    square[0:t, :] = jnp.where(
        lane == 0, sum_out, jnp.where(lane == 1, sum_head, jnp.where(lane == 2, sum_mid, 0.0))
    )
    stat[c] = jnp.transpose(square[...])[0:8, :]

    @pl.when(off_diagonal)
    def _():
        pl.semaphore_wait(barrier, 28)

    @pl.when(jnp.logical_and(diagonal, x != 0))
    def _():
        pl.semaphore_wait(barrier, 26)

    @pl.when(own_sum)
    def _():
        pl.semaphore_wait(barrier, 24)

    stat_recv = {}
    for step in (4, 5, 3, 6, 2, 7, 1):
        stat_recv[step] = new_recv()
        send_same(stat.at[c], (r, lax.rem(c + step, 8)), stat_recv[step])
    perm_recv, perm_head = new_recv(), new_recv()
    send(block_hbm, tile.at[k, j], perm_to(y), perm_recv, off_diagonal)
    send(head, head_j, perm_to(y), perm_head, off_diagonal)

    @pl.when(diagonal)
    def _():
        tile[k, j] = blk[...]
        head_j[...] = head[...]

    gate_recv, up_recv, wd_recv, wg_recv, wu_recv = (new_recv() for _ in range(5))
    send(gate_hbm.at[:, other_half], gx.at[k], sibling, gate_recv)
    send(up_hbm.at[:, other_half], ux.at[k], sibling, up_recv)
    send(w_down.at[other_half, :], wd.at[k], sibling, wd_recv)

    for copy in halves:
        copy.wait()
    arrived(gx.at[k1], gate_recv)
    arrived(ux.at[k1], up_recv)
    for q in range(2):

        @pl.loop(0, t // 16)
        def _(i):
            rows = pl.ds(hint(i * 16, 16), 16)
            out_rows = pl.ds(hint(q * t + i * 16, 16), 16)
            gate, up = gx[q, rows, :].astype(F32), ux[q, rows, :].astype(F32)
            sig = jax.nn.sigmoid(gate)
            silu = gate * sig
            fa[out_rows, :] = up * sig * (1.0 + gate * (1.0 - sig))
            fb[out_rows, :] = silu
            hid_own[out_rows, :] = (silu * up).astype(BF16)

    def hid_slot(slot, rows=None):
        size = 2 * t if rows is None else t
        return hid.at[pl.ds(hint(slot * 2 * t + (rows or 0), 16), size), own_half]

    hid_recv = [new_recv() for _ in range(10)]
    hid_sib = []

    def hid_to_sibling(slot):
        hid_sib.append((slot, new_recv()))
        send_same(hid_slot(slot), sibling, hid_sib[-1][1])

    own_hid = fetch(hid_own, hid_slot(slot_own))
    send(hid_own, hid_slot(slot_own), right, hid_recv[1])
    send(hid_own, hid_slot(slot_own), left, hid_recv[2])

    for step in (1, 7, 2, 6, 3, 5, 4):
        arrived(stat.at[lax.rem(c + 8 - step, 8)], stat_recv[step])
    total = stat[0]
    for i in range(1, 8):
        total = total + stat[i]
    total = total[:, 0:t]
    inverse_out = lax.rsqrt(total[0:1] / model + EPSILON)
    value = inverse_out * total[1:2]
    live = msk[...].astype(F32)
    slope = inverse_out * (live * (value - ret[...]))
    pack[0:1, 0:t] = slope
    pack[1:2, 0:t] = -slope * inverse_out * value / model
    pack[2:3, 0:t] = live
    pack[3:4, 0:t] = lax.rsqrt(total[2:3] / model + EPSILON)
    own_share = pl.ds(hint(8 * r, 8), 8)
    share[own_share, :] = pack[...]
    share_recv = {}
    for step in (8, 9, 7, 10, 6, 11, 5, 12, 4, 13, 3, 14, 2, 15, 1):
        share_recv[step] = new_recv()
        send_same(share.at[own_share], (lax.rem(r + step, 16), c), share_recv[step])

    sib_tile = []

    def tile_to_sibling(slot):
        sib_tile.append((slot, new_recv()))
        send_same(tile.at[k, slot], sibling, sib_tile[-1][1])

    t_part, t_own_m, t_own_p, t_oth_m, t_oth_p, t_far_own, t_far_oth = (new_recv() for _ in range(7))

    @pl.when(off_diagonal)
    def _():
        arrived(tile.at[k, c], perm_recv)
        arrived(head_j, perm_head)

    send_same(tile.at[k, c], z_partner, t_part)
    send_same(tile.at[k, c], z_plus, t_own_m)
    send_same(tile.at[k, c], z_minus, t_own_p)
    tile_to_sibling(c)
    send(hid_own, hid_slot(slot_own), partner, hid_recv[0])

    weights_down.wait()
    arrived(wd.at[k1], wd_recv)
    u_tile = 256 if half % 256 == 0 else 128
    for q in range(2):

        @pl.loop(0, half // u_tile)
        def _(n):
            units = pl.ds(hint(n * u_tile, 128), u_tile)
            wdt[q * feat : (q + 1) * feat, units] = jnp.transpose(wd[q, units, :])

    arrived(tile.at[k, 2 * zm + b], t_own_m)
    send_same(tile.at[k, 2 * zm + b], z_plus, t_far_own)
    tile_to_sibling(2 * zm + b)
    arrived(tile.at[k, 2 * z + b1], t_part)
    send_same(tile.at[k, 2 * z + b1], z_plus, t_oth_m)
    send_same(tile.at[k, 2 * z + b1], z_minus, t_oth_p)
    tile_to_sibling(2 * z + b1)
    arrived(tile.at[k, 2 * zp + b], t_own_p)
    tile_to_sibling(2 * zp + b)

    arrived(tile.at[k, 2 * zp + b1], t_oth_p)
    send_same(tile.at[k, 2 * zp + b1], z_minus, t_far_oth)
    tile_to_sibling(2 * zp + b1)
    arrived(tile.at[k, 2 * zm + b1], t_oth_m)
    tile_to_sibling(2 * zm + b1)
    arrived(hid_slot(slot_l), hid_recv[1])
    send_same(hid_slot(slot_l, 0), right, hid_recv[3])
    send_same(hid_slot(slot_l, t), partner, hid_recv[8])
    arrived(hid_slot(slot_r), hid_recv[2])
    send_same(hid_slot(slot_r, t), left, hid_recv[4])
    send_same(hid_slot(slot_r, t), partner, hid_recv[9])
    arrived(tile.at[k, 2 * zf + b], t_far_own)
    tile_to_sibling(2 * zf + b)

    for step in (1, 15, 2, 14, 3, 13, 4, 12, 5, 11, 6, 10, 7, 9, 8):
        from_row = lax.rem(r + 16 - step, 16)
        arrived(share.at[pl.ds(hint(8 * from_row, 8), 8)], share_recv[step])
    shares = share[...]
    which = lax.rem(lax.broadcasted_iota(jnp.int32, (128, 128), 0), 8)
    count = jnp.sum(jnp.sum(jnp.where(which == 2, shares, 0.0), axis=0, keepdims=True), axis=1, keepdims=True)
    factor = tokens * math.sqrt(model) / count
    columns = jnp.transpose(shares) * factor
    square[0:8, :] = pack[...]
    own_columns = jnp.transpose(square[...])

    arrived(tile.at[k, 2 * zf + b1], t_far_oth)
    tile_to_sibling(2 * zf + b1)
    send(w_gate.at[:, other_half], wg.at[own_rows], sibling, wg_recv)
    send(w_up.at[:, other_half], wu.at[own_rows], sibling, wu_recv)
    arrived(hid_slot(slot_part), hid_recv[0])
    send_same(hid_slot(slot_part, 0), right, hid_recv[5])
    send_same(hid_slot(slot_part, 0), left, hid_recv[6])
    for slot, sem in sib_tile:
        arrived(tile.at[k1, slot], sem)

    head_row = head_j[...]
    for s in range(8):
        for q in range(2):
            at = 8 * (2 * s + q)
            dout[(2 * s + q) * t : (2 * s + q + 1) * t, :] = (
                columns[0:t, at : at + 1] * head_row + columns[0:t, at + 1 : at + 2] * tile[q, s].astype(F32)
            ).astype(BF16)

    def chunk(slot, piece, start=0, size=2 * t):
        return part_sum.at[pl.ds(hint(slot * 2 * t + start, 16), size), piece]

    def hidden(slot, piece):
        rows = pl.ds(hint(slot * 2 * t, 16), 2 * t)
        part_sum[rows, piece] = dot(dout[rows, :], wdt[:, piece]).astype(BF16)

    def add_into(slot, piece, others, start=0, size=2 * t):
        @pl.loop(0, size // 16)
        def _(i):
            rows = pl.ds(hint(slot * 2 * t + start + i * 16, 16), 16)
            their = pl.ds(hint(i * 16, 16), 16)
            value = part_sum[rows, piece].astype(F32)
            for other in others:
                value = value + other[their, piece].astype(F32)
            part_sum[rows, piece] = value.astype(BF16)

    both = (0, 1)
    rf_s, nl_s, nr_s, ha_s, hb_s, ml_s, mr_s, my_s = ([new_recv(), new_recv()] for _ in range(8))
    for h in both:
        hidden(slot_fo, pieces[h])
        send(chunk(slot_fo, pieces[h]), rf.at[:, pieces[h]], partner, rf_s[h])
        hidden(slot_ro, pieces[h])
        send(chunk(slot_ro, pieces[h]), nl.at[:, pieces[h]], right, nl_s[h])
        hidden(slot_lo, pieces[h])
        send(chunk(slot_lo, pieces[h]), nr.at[:, pieces[h]], left, nr_s[h])
    for h in both:
        hidden(slot_f, pieces[h])
        arrived(rf.at[:, pieces[h]], rf_s[h])
        add_into(slot_f, pieces[h], (rf,))
        send(chunk(slot_f, pieces[h], 0, t), ha.at[:, pieces[h]], right, ha_s[h])
        send(chunk(slot_f, pieces[h], t, t), hb.at[:, pieces[h]], left, hb_s[h])
    for h in both:
        hidden(slot_part, pieces[h])
    for h in both:
        hidden(slot_r, pieces[h])
        hidden(slot_l, pieces[h])
        arrived(nl.at[:, pieces[h]], nl_s[h])
        arrived(nr.at[:, pieces[h]], nr_s[h])
        add_into(slot_part, pieces[h], (nl, nr))
        send(chunk(slot_part, pieces[h]), my.at[:, pieces[h]], partner, my_s[h])
    for h in both:
        arrived(ha.at[:, pieces[h]], ha_s[h])
        add_into(slot_r, pieces[h], (ha,), 0, t)
        send(chunk(slot_r, pieces[h]), ml.at[:, pieces[h]], right, ml_s[h])
        arrived(hb.at[:, pieces[h]], hb_s[h])
        add_into(slot_l, pieces[h], (hb,), t, t)
        send(chunk(slot_l, pieces[h]), mr.at[:, pieces[h]], left, mr_s[h])
    for h in both:
        hidden(slot_own, pieces[h])

    arrived(hid_slot(slot_f, 0), hid_recv[3])
    arrived(hid_slot(slot_f, t), hid_recv[4])
    send_same(hid_slot(slot_f), partner, hid_recv[7])
    own_hid.wait()
    arrived(hid_slot(slot_lo, 0), hid_recv[5])
    arrived(hid_slot(slot_ro, 0), hid_recv[6])
    arrived(hid_slot(slot_lo, t), hid_recv[8])
    arrived(hid_slot(slot_ro, t), hid_recv[9])
    for slot in (slot_own, slot_l, slot_r, slot_part, slot_f, slot_lo, slot_ro):
        hid_to_sibling(slot)
    for copy in weights_in:
        copy.wait()
    other_rows = pl.ds(hint(k1 * feat, 16), feat)
    f_tile = 256 if width % 256 == 0 else 128
    for source, target, sem in ((wg, wgt, wg_recv), (wu, wut, wu_recv)):
        arrived(source.at[other_rows], sem)

        @pl.loop(0, width // f_tile)
        def _(n):
            features = pl.ds(hint(n * f_tile, 128), f_tile)
            target[:, features] = jnp.transpose(source[features, :])

    inverse_mid_column = own_columns[0:t, 3:4]
    outv[...] = (
        (own_columns[0:t, 0:1] * factor) * head[...] + (own_columns[0:t, 1:2] * factor) * blk[...].astype(F32)
    ).astype(BF16)

    dg_recv = [[new_recv(), new_recv()] for _ in range(10)]
    sb_recv = [new_recv() for _ in range(8)]
    pending, last = [], []

    def whole(slot, piece):
        return dg.at[slot, :, :, piece]

    cut = 2 * t - 16

    def most(slot, piece):
        return dg.at[slot, :, 0:cut, piece]

    def rest(slot, piece):
        return dg.at[slot, :, cut:, piece]

    def one(slot, which, piece):
        return dg.at[slot, which, :, piece]

    for h in both:
        piece = pieces[h]
        arrived(my.at[:, piece], my_s[h])
        arrived(ml.at[:, piece], ml_s[h])
        arrived(mr.at[:, piece], mr_s[h])

        @pl.loop(0, 2 * t // 16)
        def _(i):
            rows = pl.ds(hint(i * 16, 16), 16)
            d_hidden = (
                part_sum[pl.ds(hint(slot_own * 2 * t + i * 16, 16), 16), piece].astype(F32)
                + ml[rows, piece].astype(F32)
                + mr[rows, piece].astype(F32)
                + my[rows, piece].astype(F32)
            )
            dg[slot_own, 0, rows, piece] = (d_hidden * fa[rows, piece]).astype(BF16)
            dg[slot_own, 1, rows, piece] = (d_hidden * fb[rows, piece]).astype(BF16)

        send_same(whole(slot_own, piece), right, dg_recv[1][h])
        send_same(whole(slot_own, piece), left, dg_recv[2][h])
        send_same(whole(slot_own, piece), partner, dg_recv[0][h])

    def product(slot, h):
        piece = pieces[h]
        value = dot(dg[slot, 0, :, piece], wgt[piece, :]) + dot(dg[slot, 1, :, piece], wut[piece, :])
        if h == 0:
            yf[slot] = value
            return
        value = value + yf[slot]
        yf[slot] = value
        yb[slot] = value.astype(BF16)
        sem = sb_recv[len(last) + len(pending)]
        send(yb.at[slot, pl.ds(hint(k1 * t, 16), t)], sb.at[slot], sibling, sem)
        pending.append((slot, sem))

    def combine():
        slot, sem = pending.pop(0)
        arrived(sb.at[slot], sem)
        zz, bb = lax.rem(lax.div(slot, 2) + x, 4), lax.rem(slot, 2)
        summed = (yf[slot, pl.ds(hint(k * t, 16), t), :] + sb[slot].astype(F32)).astype(BF16)
        zs[slot] = summed
        send(zs.at[slot], zr.at[bb, z], (r, 2 * zz + b), z_sems.at[bb, z], zz != z)

        @pl.when(zz == z)
        def _():
            zr[bb, z] = summed

        last.append(slot)

    def over_z(q):
        for step in range(1, 4):
            zz = lax.rem(z + step, 4)
            arrived(zr.at[q, zz], z_sems.at[q, zz])
        vs[q] = (
            zr[q, 0].astype(F32) + zr[q, 1].astype(F32) + zr[q, 2].astype(F32) + zr[q, 3].astype(F32)
        ).astype(BF16)

    def d_w_down(source, part):
        @pl.loop(0, half // u_tile)
        def _(n):
            units = pl.ds(hint(n * u_tile, 128), u_tile)
            wd[part, units, :] = lax.dot_general(
                source[0:tokens, units],
                dout[:, pl.ds(hint(k * feat, 128), feat)],
                (((0,), (0,)), ((), ())),
                preferred_element_type=F32,
            ).astype(BF16)

        part_rows = pl.ds(hint(part * half, 16), half)
        return fetch(wd.at[part], dw_hbm.at[part_rows, :])

    product(slot_own, 0)
    product(slot_own, 1)
    arrived(hid_slot(slot_fo), hid_recv[7])
    hid_to_sibling(slot_fo)
    fetch(hid.at[:, own_half], wg.at[0:tokens]).wait()
    own_dw = d_w_down(wg, k)
    for h in both:
        arrived(whole(slot_l, pieces[h]), dg_recv[1][h])
        send_same(one(slot_l, 0, pieces[h]), right, dg_recv[3][h])
        send_same(rest(slot_l, pieces[h]), partner, dg_recv[8][h])
        arrived(whole(slot_r, pieces[h]), dg_recv[2][h])
        send_same(one(slot_r, 1, pieces[h]), left, dg_recv[4][h])
        send_same(rest(slot_r, pieces[h]), partner, dg_recv[9][h])
        if h == 0:
            combine()
            product(slot_l, 0)
            product(slot_r, 0)
            for slot, sem in hid_sib:
                arrived(hid.at[pl.ds(hint(slot * 2 * t, 16), 2 * t), other_half], sem)
            fetch(hid.at[:, other_half], wu.at[0:tokens]).wait()
            other_dw = d_w_down(wu, k1)
    for h in both:
        arrived(whole(slot_part, pieces[h]), dg_recv[0][h])
        send_same(most(slot_part, pieces[h]), right, dg_recv[5][h])
        send_same(most(slot_part, pieces[h]), left, dg_recv[6][h])
    product(slot_l, 1)
    product(slot_r, 1)
    for h in both:
        arrived(one(slot_f, 0, pieces[h]), dg_recv[3][h])
        arrived(one(slot_f, 1, pieces[h]), dg_recv[4][h])
        send_same(whole(slot_f, pieces[h]), partner, dg_recv[7][h])
        if h == 0:
            combine()
            product(slot_part, 0)
            product(slot_part, 1)
            combine()
        product(slot_f, h)
    combine()
    combine()

    same = lax.rem(y + b, 2)
    over_z(y)
    send(vs.at[y], dn.at[same], sum_to(y), d_sems.at[same], not_own_sum)

    @pl.when(own_sum)
    def _():
        dn[same] = vs[y]

    for h in both:
        arrived(whole(slot_fo, pieces[h]), dg_recv[7][h])
        product(slot_fo, h)
        arrived(most(slot_lo, pieces[h]), dg_recv[5][h])
        arrived(rest(slot_lo, pieces[h]), dg_recv[8][h])
        product(slot_lo, h)
        arrived(most(slot_ro, pieces[h]), dg_recv[6][h])
        arrived(rest(slot_ro, pieces[h]), dg_recv[9][h])
        product(slot_ro, h)
    combine()
    combine()
    combine()
    over_z(y1)
    send(vs.at[y1], dn.at[1 - same], sum_to(y1), d_sems.at[1 - same])

    @pl.when(not_own_sum)
    def _():
        arrived(dn.at[0], d_sems.at[0])

    arrived(dn.at[1], d_sems.at[1])
    scaled = (dn[0].astype(F32) + dn[1].astype(F32)) * gains[2]
    normed = mid[...].astype(F32) * inverse_mid_column
    inner = jnp.sum(scaled * normed, axis=1, keepdims=True)
    square[0:t, :] = jnp.broadcast_to(inner, (t, 128))
    fin[c] = jnp.transpose(square[...])[0:8, :]
    fin_recv = {}
    for step in (4, 5, 3, 6, 2, 7, 1):
        fin_recv[step] = new_recv()
        send_same(fin.at[c], (r, lax.rem(c + step, 8)), fin_recv[step])
    for step in (1, 7, 2, 6, 3, 5, 4):
        arrived(fin.at[lax.rem(c + 8 - step, 8)], fin_recv[step])
    total = fin[0]
    for i in range(1, 8):
        total = total + fin[i]
    square[0:8, :] = total
    inner_column = jnp.transpose(square[...])[0:t, 0:1]
    outv[...] = (
        outv[...].astype(F32) + inverse_mid_column * (scaled - normed * (inner_column / model))
    ).astype(BF16)
    final = fetch(outv, out_hbm)
    own_dw.wait()
    other_dw.wait()
    final.wait()
    for copy, when in sent:
        if when is None:
            copy.wait_send()
        else:
            pl.when(when)(copy.wait_send)


def widen(narrow, wide):
    wide[...] = narrow[...].astype(F32)


def local(
    block_out, stream_mid, gate_pre, up_pre, final_gain, mlp_gain, value_weight, returns, response_mask, w_gate, w_up, w_down
):
    t, width = block_out.shape
    units = gate_pre.shape[1]
    half, feat = units // 2, width // 2
    any_spec = pl.BlockSpec(memory_space=pl.ANY)
    vm = pltpu.VMEM
    out, _, d_w_down = pl.pallas_call(
        kernel,
        out_shape=(
            jax.ShapeDtypeStruct((t, width), BF16),
            jax.ShapeDtypeStruct((16 * t, units), BF16),
            jax.ShapeDtypeStruct((units, feat), BF16),
        ),
        in_specs=[any_spec] * 12,
        out_specs=(any_spec,) * 3,
        scratch_shapes=[
            vm((t, width), BF16),
            vm((t, width), BF16),
            vm((3, 1, width), F32),
            vm((1, t), F32),
            vm((1, t), jnp.int32),
            vm((8, 128), F32),
            vm((2, t, half), BF16),
            vm((2, t, half), BF16),
            vm((2, half, feat), BF16),
            vm((width, half), BF16),
            vm((width, half), BF16),
            vm((width, half), BF16),
            vm((half, width), BF16),
            vm((half, width), BF16),
            vm((2 * t, half), F32),
            vm((2 * t, half), F32),
            vm((2 * t, half), BF16),
            vm((128, 128), F32),
            vm((8, 8, 128), F32),
            vm((128, 128), F32),
            vm((2, 8, t, width), BF16),
            vm((1, width), F32),
            vm((1, width), F32),
            vm((16 * t, width), BF16),
            vm((16 * t, half), BF16),
            vm((2 * t, half), BF16),
            vm((2 * t, half), BF16),
            vm((2 * t, half), BF16),
            vm((t, half), BF16),
            vm((t, half), BF16),
            vm((2 * t, half), BF16),
            vm((2 * t, half), BF16),
            vm((2 * t, half), BF16),
            vm((8, 2, 2 * t, half), BF16),
            vm((8, 2 * t, width), F32),
            vm((8, 2 * t, width), BF16),
            vm((8, t, width), BF16),
            vm((8, t, width), BF16),
            vm((2, 4, t, width), BF16),
            vm((2, t, width), BF16),
            vm((2, t, width), BF16),
            vm((8, 8, 128), F32),
            vm((t, width), BF16),
            pltpu.SemaphoreType.DMA((N_SEND,)),
            pltpu.SemaphoreType.DMA((N_RECV,)),
            pltpu.SemaphoreType.DMA((N_LOCAL,)),
            pltpu.SemaphoreType.DMA((2, 4)),
            pltpu.SemaphoreType.DMA((2,)),
        ],
        compiler_params=pltpu.CompilerParams(
            collective_id=0, has_side_effects=True, vmem_limit_bytes=60 * 1024 * 1024
        ),
    )(
        block_out, stream_mid, gate_pre, up_pre,
        final_gain.reshape(1, width), mlp_gain.reshape(1, width), value_weight.reshape(1, width),
        returns.reshape(1, t), response_mask.reshape(1, t), w_gate, w_up, w_down,
    )
    rows = units // 7 if units % (7 * 16) == 0 else units
    spec = pl.BlockSpec((rows, feat), lambda i: (i, 0))
    d_w_down = pl.pallas_call(
        widen,
        out_shape=jax.ShapeDtypeStruct((units, feat), F32),
        grid=(units // rows,),
        in_specs=[spec],
        out_specs=spec,
    )(d_w_down)
    return out, d_w_down


def solution(mesh):
    placed = (
        P("row", "col"), P("row", "col"), P("row", "col"), P("row", "col"),
        P("col"), P("col"), P("col"), P("row"), P("row"),
        P("row", "col"), P("row", "col"), P("col", "row"),
    )
    return jax.shard_map(
        local, mesh=mesh, in_specs=placed, out_specs=(P("row", "col"), P("col", "row")), check_vma=False
    )
```

```python
import functools
import math

import jax
import jax.numpy as jnp
from jax import lax
from jax.experimental import pallas as pl
from jax.experimental.pallas import tpu as pltpu
from jax.sharding import PartitionSpec as P

EPSILON = 1e-05
MESH = pl.DeviceIdType.MESH
F32 = jnp.float32
BF16 = jnp.bfloat16


def dot(left, right):
    return lax.dot_general(left, right, (((1,), (0,)), ((), ())), preferred_element_type=F32)


def hint(value, factor):
    return pl.multiple_of(value, factor)


class Sems:
    def __init__(self, ref):
        self.ref, self.used = ref, 0

    def __call__(self):
        self.used += 1
        return self.ref.at[self.used - 1]


N_SEND, N_RECV, N_LOCAL = 160, 160, 24


def kernel(
    block_hbm, mid_hbm, gate_hbm, up_hbm, final_gain, mlp_gain, value_weight, returns, mask, w_gate, w_up, w_down,
    out_hbm, hid, dw_hbm,
    blk, mid, gains, ret, msk, pack, gx, ux, wd, wg, wu, wdt, wgt, wut, fa, fb, hid_own,
    square, stat, share, tile, head, head_j, dout, part_sum,
    rf, nl, nr, ha, hb, ml, mr, my, dg, yf, yb, sb, zs, zr, vs, dn, fin, outv,
    send_sems, recv_sems, local_sems, z_sems, d_sems,
):
    t, width = blk.shape
    half = gx.shape[2]
    feat = width // 2
    tokens = 16 * t
    model = 8 * width
    first = (half // 2 + 255) // 256 * 256 if half >= 512 else half // 2
    pieces = (pl.ds(0, first), pl.ds(first, half - first))
    r, c = lax.axis_index("row"), lax.axis_index("col")
    k, j = lax.rem(r, 2), lax.div(r, 2)
    x, y = lax.div(j, 2), lax.rem(j, 2)
    z, b = lax.div(c, 2), lax.rem(c, 2)
    k1, y1, b1 = 1 - k, 1 - y, 1 - b
    xr, xl, xf = lax.rem(x + 1, 4), lax.rem(x + 3, 4), lax.rem(x + 2, 4)
    zp, zm, zf = lax.rem(z + 1, 4), lax.rem(z + 3, 4), lax.rem(z + 2, 4)
    sibling = (2 * j + k1, c)
    right, left = (4 * xr + 2 * y + k, c), (4 * xl + 2 * y + k, c)
    partner = (4 * x + 2 * y1 + k, c)
    z_plus, z_minus, z_partner = (r, 2 * zp + b), (r, 2 * zm + b), (r, 2 * z + b1)
    slot_own, slot_part = 2 * x + y, 2 * x + y1
    slot_l, slot_r, slot_f = 2 * xl + y, 2 * xr + y, 2 * xf + y
    slot_lo, slot_ro, slot_fo = 2 * xl + y1, 2 * xr + y1, 2 * xf + y1
    own_half = pl.ds(hint(k * half, 128), half)
    other_half = pl.ds(hint(k1 * half, 128), half)
    diagonal = j == c
    off_diagonal = j != c
    new_send, new_recv, new_local = Sems(send_sems), Sems(recv_sems), Sems(local_sems)
    sent = []

    def send(src, dst, to, recv, when=None):
        copy = pltpu.make_async_remote_copy(
            src_ref=src, dst_ref=dst, send_sem=new_send(), recv_sem=recv, device_id=to, device_id_type=MESH
        )
        if when is None:
            copy.start()
        else:
            pl.when(when)(copy.start)
        sent.append((copy, when))

    def send_same(ref, to, recv):
        send(ref, ref, to, recv)

    def arrived(dst, recv):
        pltpu.make_async_copy(dst, dst, recv).wait()

    def fetch(src, dst):
        copy = pltpu.make_async_copy(src, dst, new_local())
        copy.start()
        return copy

    barrier = pltpu.get_barrier_semaphore()

    def greet(device):
        pl.semaphore_signal(barrier, inc=1, device_id=device, device_id_type=MESH)

    def perm_to(which):
        return (2 * c + k, 2 * x + which)

    def perm_from():
        return (2 * c + k, j)

    sum_x = lax.rem(z + 4 - x, 4)
    own_sum = jnp.logical_and(diagonal, x == 0)
    not_own_sum = jnp.logical_not(own_sum)

    def sum_to(which):
        return (2 * (2 * sum_x + which) + k, j)

    def sum_from(which):
        return (2 * c + k, 2 * lax.rem(x + z, 4) + which)

    greet(sum_to(b1))
    greet(sum_from(y1))

    @pl.when(not_own_sum)
    def _():
        greet(sum_to(b))
        greet(sum_from(y))

    @pl.when(off_diagonal)
    def _():
        greet(perm_to(y))
        greet(perm_from())

    for step in (4, 5, 3, 6, 2, 7, 1):
        greet((r, lax.rem(c + step, 8)))
    for step in (8, 9, 7, 10, 6, 11, 5, 12, 4, 13, 3, 14, 2, 15, 1):
        greet((lax.rem(r + step, 16), c))

    small = [
        fetch(block_hbm, blk),
        fetch(mid_hbm, mid),
        fetch(final_gain, gains.at[0]),
        fetch(value_weight, gains.at[1]),
        fetch(mlp_gain, gains.at[2]),
        fetch(returns, ret),
        fetch(mask, msk),
    ]
    halves = [fetch(gate_hbm.at[:, own_half], gx.at[k]), fetch(up_hbm.at[:, own_half], ux.at[k])]
    own_rows = pl.ds(hint(k * feat, 16), feat)
    weights_down = fetch(w_down.at[own_half, :], wd.at[k])
    weights_in = [fetch(w_gate.at[:, own_half], wg.at[own_rows]), fetch(w_up.at[:, own_half], wu.at[own_rows])]
    for copy in small:
        copy.wait()

    lane = lax.broadcasted_iota(jnp.int32, (t, 128), 1)
    head[...] = gains[0] * gains[1]
    block_wide = blk[...].astype(F32)
    mid_wide = mid[...].astype(F32)
    square[...] = jnp.zeros_like(square)
    pack[...] = jnp.zeros_like(pack)
    sum_out = jnp.sum(block_wide * block_wide, axis=1, keepdims=True)
    sum_head = jnp.sum(block_wide * head[...], axis=1, keepdims=True)
    sum_mid = jnp.sum(mid_wide * mid_wide, axis=1, keepdims=True)
    square[0:t, :] = jnp.where(
        lane == 0, sum_out, jnp.where(lane == 1, sum_head, jnp.where(lane == 2, sum_mid, 0.0))
    )
    stat[c] = jnp.transpose(square[...])[0:8, :]

    @pl.when(off_diagonal)
    def _():
        pl.semaphore_wait(barrier, 28)

    @pl.when(jnp.logical_and(diagonal, x != 0))
    def _():
        pl.semaphore_wait(barrier, 26)

    @pl.when(own_sum)
    def _():
        pl.semaphore_wait(barrier, 24)

    stat_recv = {}
    for step in (4, 5, 3, 6, 2, 7, 1):
        stat_recv[step] = new_recv()
        send_same(stat.at[c], (r, lax.rem(c + step, 8)), stat_recv[step])
    perm_recv, perm_head = new_recv(), new_recv()
    send(block_hbm, tile.at[k, j], perm_to(y), perm_recv, off_diagonal)
    send(head, head_j, perm_to(y), perm_head, off_diagonal)

    @pl.when(diagonal)
    def _():
        tile[k, j] = blk[...]
        head_j[...] = head[...]

    gate_recv, up_recv, wd_recv, wg_recv, wu_recv = (new_recv() for _ in range(5))
    send(gate_hbm.at[:, other_half], gx.at[k], sibling, gate_recv)
    send(up_hbm.at[:, other_half], ux.at[k], sibling, up_recv)
    send(w_down.at[other_half, :], wd.at[k], sibling, wd_recv)

    for copy in halves:
        copy.wait()
    arrived(gx.at[k1], gate_recv)
    arrived(ux.at[k1], up_recv)
    for q in range(2):

        @pl.loop(0, t // 16)
        def _(i):
            rows = pl.ds(hint(i * 16, 16), 16)
            out_rows = pl.ds(hint(q * t + i * 16, 16), 16)
            gate, up = gx[q, rows, :].astype(F32), ux[q, rows, :].astype(F32)
            sig = jax.nn.sigmoid(gate)
            silu = gate * sig
            fa[out_rows, :] = up * sig * (1.0 + gate * (1.0 - sig))
            fb[out_rows, :] = silu
            hid_own[out_rows, :] = (silu * up).astype(BF16)

    def hid_slot(slot, rows=None):
        size = 2 * t if rows is None else t
        return hid.at[pl.ds(hint(slot * 2 * t + (rows or 0), 16), size), own_half]

    hid_recv = [new_recv() for _ in range(10)]
    hid_sib = []

    def hid_to_sibling(slot):
        hid_sib.append((slot, new_recv()))
        send_same(hid_slot(slot), sibling, hid_sib[-1][1])

    own_hid = fetch(hid_own, hid_slot(slot_own))
    send(hid_own, hid_slot(slot_own), right, hid_recv[1])
    send(hid_own, hid_slot(slot_own), left, hid_recv[2])

    for step in (1, 7, 2, 6, 3, 5, 4):
        arrived(stat.at[lax.rem(c + 8 - step, 8)], stat_recv[step])
    total = stat[0]
    for i in range(1, 8):
        total = total + stat[i]
    total = total[:, 0:t]
    inverse_out = lax.rsqrt(total[0:1] / model + EPSILON)
    value = inverse_out * total[1:2]
    live = msk[...].astype(F32)
    slope = inverse_out * (live * (value - ret[...]))
    pack[0:1, 0:t] = slope
    pack[1:2, 0:t] = -slope * inverse_out * value / model
    pack[2:3, 0:t] = live
    pack[3:4, 0:t] = lax.rsqrt(total[2:3] / model + EPSILON)
    own_share = pl.ds(hint(8 * r, 8), 8)
    share[own_share, :] = pack[...]
    share_recv = {}
    for step in (8, 9, 7, 10, 6, 11, 5, 12, 4, 13, 3, 14, 2, 15, 1):
        share_recv[step] = new_recv()
        send_same(share.at[own_share], (lax.rem(r + step, 16), c), share_recv[step])

    sib_tile = []

    def tile_to_sibling(slot):
        sib_tile.append((slot, new_recv()))
        send_same(tile.at[k, slot], sibling, sib_tile[-1][1])

    t_part, t_own_m, t_own_p, t_oth_m, t_oth_p, t_far_own, t_far_oth = (new_recv() for _ in range(7))

    @pl.when(off_diagonal)
    def _():
        arrived(tile.at[k, c], perm_recv)
        arrived(head_j, perm_head)

    send_same(tile.at[k, c], z_partner, t_part)
    send_same(tile.at[k, c], z_plus, t_own_m)
    send_same(tile.at[k, c], z_minus, t_own_p)
    tile_to_sibling(c)
    send(hid_own, hid_slot(slot_own), partner, hid_recv[0])

    weights_down.wait()
    arrived(wd.at[k1], wd_recv)
    u_tile = 256 if half % 256 == 0 else 128
    for q in range(2):

        @pl.loop(0, half // u_tile)
        def _(n):
            units = pl.ds(hint(n * u_tile, 128), u_tile)
            wdt[q * feat : (q + 1) * feat, units] = jnp.transpose(wd[q, units, :])

    arrived(tile.at[k, 2 * zm + b], t_own_m)
    send_same(tile.at[k, 2 * zm + b], z_plus, t_far_own)
    tile_to_sibling(2 * zm + b)
    arrived(tile.at[k, 2 * z + b1], t_part)
    send_same(tile.at[k, 2 * z + b1], z_plus, t_oth_m)
    send_same(tile.at[k, 2 * z + b1], z_minus, t_oth_p)
    tile_to_sibling(2 * z + b1)
    arrived(tile.at[k, 2 * zp + b], t_own_p)
    tile_to_sibling(2 * zp + b)
    arrived(hid_slot(slot_l), hid_recv[1])
    send_same(hid_slot(slot_l, 0), right, hid_recv[3])
    send_same(hid_slot(slot_l, t), partner, hid_recv[8])
    arrived(hid_slot(slot_r), hid_recv[2])
    send_same(hid_slot(slot_r, t), left, hid_recv[4])
    send_same(hid_slot(slot_r, t), partner, hid_recv[9])

    arrived(tile.at[k, 2 * zp + b1], t_oth_p)
    send_same(tile.at[k, 2 * zp + b1], z_minus, t_far_oth)
    tile_to_sibling(2 * zp + b1)
    arrived(tile.at[k, 2 * zm + b1], t_oth_m)
    tile_to_sibling(2 * zm + b1)
    arrived(tile.at[k, 2 * zf + b], t_far_own)
    tile_to_sibling(2 * zf + b)

    for step in (1, 15, 2, 14, 3, 13, 4, 12, 5, 11, 6, 10, 7, 9, 8):
        from_row = lax.rem(r + 16 - step, 16)
        arrived(share.at[pl.ds(hint(8 * from_row, 8), 8)], share_recv[step])
    shares = share[...]
    which = lax.rem(lax.broadcasted_iota(jnp.int32, (128, 128), 0), 8)
    count = jnp.sum(jnp.sum(jnp.where(which == 2, shares, 0.0), axis=0, keepdims=True), axis=1, keepdims=True)
    factor = tokens * math.sqrt(model) / count
    columns = jnp.transpose(shares) * factor
    square[0:8, :] = pack[...]
    own_columns = jnp.transpose(square[...])

    arrived(tile.at[k, 2 * zf + b1], t_far_oth)
    tile_to_sibling(2 * zf + b1)
    send(w_gate.at[:, other_half], wg.at[own_rows], sibling, wg_recv)
    send(w_up.at[:, other_half], wu.at[own_rows], sibling, wu_recv)
    arrived(hid_slot(slot_part), hid_recv[0])
    send_same(hid_slot(slot_part, 0), right, hid_recv[5])
    send_same(hid_slot(slot_part, 0), left, hid_recv[6])
    for slot, sem in sib_tile:
        arrived(tile.at[k1, slot], sem)

    head_row = head_j[...]
    for s in range(8):
        for q in range(2):
            at = 8 * (2 * s + q)
            dout[(2 * s + q) * t : (2 * s + q + 1) * t, :] = (
                columns[0:t, at : at + 1] * head_row + columns[0:t, at + 1 : at + 2] * tile[q, s].astype(F32)
            ).astype(BF16)

    def chunk(slot, piece, start=0, size=2 * t):
        return part_sum.at[pl.ds(hint(slot * 2 * t + start, 16), size), piece]

    def hidden(slot, piece):
        rows = pl.ds(hint(slot * 2 * t, 16), 2 * t)
        part_sum[rows, piece] = dot(dout[rows, :], wdt[:, piece]).astype(BF16)

    def add_into(slot, piece, others, start=0, size=2 * t):
        @pl.loop(0, size // 16)
        def _(i):
            rows = pl.ds(hint(slot * 2 * t + start + i * 16, 16), 16)
            their = pl.ds(hint(i * 16, 16), 16)
            value = part_sum[rows, piece].astype(F32)
            for other in others:
                value = value + other[their, piece].astype(F32)
            part_sum[rows, piece] = value.astype(BF16)

    both = (0, 1)
    rf_s, nl_s, nr_s, ha_s, hb_s, ml_s, mr_s, my_s = ([new_recv(), new_recv()] for _ in range(8))
    for h in both:
        hidden(slot_fo, pieces[h])
        send(chunk(slot_fo, pieces[h]), rf.at[:, pieces[h]], partner, rf_s[h])
        hidden(slot_ro, pieces[h])
        send(chunk(slot_ro, pieces[h]), nl.at[:, pieces[h]], right, nl_s[h])
        hidden(slot_lo, pieces[h])
        send(chunk(slot_lo, pieces[h]), nr.at[:, pieces[h]], left, nr_s[h])
    arrived(hid_slot(slot_f, 0), hid_recv[3])
    arrived(hid_slot(slot_f, t), hid_recv[4])
    send_same(hid_slot(slot_f), partner, hid_recv[7])
    for h in both:
        hidden(slot_f, pieces[h])
        arrived(rf.at[:, pieces[h]], rf_s[h])
        add_into(slot_f, pieces[h], (rf,))
        send(chunk(slot_f, pieces[h], 0, t), ha.at[:, pieces[h]], right, ha_s[h])
        send(chunk(slot_f, pieces[h], t, t), hb.at[:, pieces[h]], left, hb_s[h])
    for h in both:
        hidden(slot_part, pieces[h])
    for h in both:
        hidden(slot_r, pieces[h])
        hidden(slot_l, pieces[h])
        arrived(nl.at[:, pieces[h]], nl_s[h])
        arrived(nr.at[:, pieces[h]], nr_s[h])
        add_into(slot_part, pieces[h], (nl, nr))
        send(chunk(slot_part, pieces[h]), my.at[:, pieces[h]], partner, my_s[h])
    for h in both:
        arrived(ha.at[:, pieces[h]], ha_s[h])
        add_into(slot_r, pieces[h], (ha,), 0, t)
        send(chunk(slot_r, pieces[h]), ml.at[:, pieces[h]], right, ml_s[h])
        arrived(hb.at[:, pieces[h]], hb_s[h])
        add_into(slot_l, pieces[h], (hb,), t, t)
        send(chunk(slot_l, pieces[h]), mr.at[:, pieces[h]], left, mr_s[h])
    for h in both:
        hidden(slot_own, pieces[h])

    own_hid.wait()
    arrived(hid_slot(slot_lo, 0), hid_recv[5])
    arrived(hid_slot(slot_ro, 0), hid_recv[6])
    arrived(hid_slot(slot_lo, t), hid_recv[8])
    arrived(hid_slot(slot_ro, t), hid_recv[9])
    arrived(hid_slot(slot_fo), hid_recv[7])
    for slot in (slot_own, slot_l, slot_r, slot_part, slot_f, slot_lo, slot_ro, slot_fo):
        hid_to_sibling(slot)
    for copy in weights_in:
        copy.wait()
    other_rows = pl.ds(hint(k1 * feat, 16), feat)
    f_tile = 256 if width % 256 == 0 else 128
    for source, target, sem in ((wg, wgt, wg_recv), (wu, wut, wu_recv)):
        arrived(source.at[other_rows], sem)

        @pl.loop(0, width // f_tile)
        def _(n):
            features = pl.ds(hint(n * f_tile, 128), f_tile)
            target[:, features] = jnp.transpose(source[features, :])

    inverse_mid_column = own_columns[0:t, 3:4]
    outv[...] = (
        (own_columns[0:t, 0:1] * factor) * head[...] + (own_columns[0:t, 1:2] * factor) * blk[...].astype(F32)
    ).astype(BF16)

    dg_recv = [[new_recv(), new_recv()] for _ in range(10)]
    sb_recv = [new_recv() for _ in range(8)]
    pending, last = [], []

    def whole(slot, piece):
        return dg.at[slot, :, :, piece]

    cut = 2 * t - 16

    def most(slot, piece):
        return dg.at[slot, :, 0:cut, piece]

    def rest(slot, piece):
        return dg.at[slot, :, cut:, piece]

    def one(slot, which, piece):
        return dg.at[slot, which, :, piece]

    for h in both:
        piece = pieces[h]
        arrived(my.at[:, piece], my_s[h])
        arrived(ml.at[:, piece], ml_s[h])
        arrived(mr.at[:, piece], mr_s[h])

        @pl.loop(0, 2 * t // 16)
        def _(i):
            rows = pl.ds(hint(i * 16, 16), 16)
            d_hidden = (
                part_sum[pl.ds(hint(slot_own * 2 * t + i * 16, 16), 16), piece].astype(F32)
                + ml[rows, piece].astype(F32)
                + mr[rows, piece].astype(F32)
                + my[rows, piece].astype(F32)
            )
            dg[slot_own, 0, rows, piece] = (d_hidden * fa[rows, piece]).astype(BF16)
            dg[slot_own, 1, rows, piece] = (d_hidden * fb[rows, piece]).astype(BF16)

        send_same(whole(slot_own, piece), right, dg_recv[1][h])
        send_same(whole(slot_own, piece), left, dg_recv[2][h])
        send_same(whole(slot_own, piece), partner, dg_recv[0][h])

    def product(slot, h):
        piece = pieces[h]
        value = dot(dg[slot, 0, :, piece], wgt[piece, :]) + dot(dg[slot, 1, :, piece], wut[piece, :])
        if h == 0:
            yf[slot] = value
            return
        value = value + yf[slot]
        yf[slot] = value
        yb[slot] = value.astype(BF16)
        sem = sb_recv[len(last) + len(pending)]
        send(yb.at[slot, pl.ds(hint(k1 * t, 16), t)], sb.at[slot], sibling, sem)
        pending.append((slot, sem))

    def combine():
        slot, sem = pending.pop(0)
        arrived(sb.at[slot], sem)
        zz, bb = lax.rem(lax.div(slot, 2) + x, 4), lax.rem(slot, 2)
        summed = (yf[slot, pl.ds(hint(k * t, 16), t), :] + sb[slot].astype(F32)).astype(BF16)
        zs[slot] = summed
        send(zs.at[slot], zr.at[bb, z], (r, 2 * zz + b), z_sems.at[bb, z], zz != z)

        @pl.when(zz == z)
        def _():
            zr[bb, z] = summed

        last.append(slot)

    def over_z(q):
        for step in range(1, 4):
            zz = lax.rem(z + step, 4)
            arrived(zr.at[q, zz], z_sems.at[q, zz])
        vs[q] = (
            zr[q, 0].astype(F32) + zr[q, 1].astype(F32) + zr[q, 2].astype(F32) + zr[q, 3].astype(F32)
        ).astype(BF16)

    def d_w_down(source, part):
        @pl.loop(0, half // u_tile)
        def _(n):
            units = pl.ds(hint(n * u_tile, 128), u_tile)
            wd[part, units, :] = lax.dot_general(
                source[0:tokens, units],
                dout[:, pl.ds(hint(k * feat, 128), feat)],
                (((0,), (0,)), ((), ())),
                preferred_element_type=F32,
            ).astype(BF16)

        part_rows = pl.ds(hint(part * half, 16), half)
        return fetch(wd.at[part], dw_hbm.at[part_rows, :])

    product(slot_own, 0)
    product(slot_own, 1)
    fetch(hid.at[:, own_half], wg.at[0:tokens]).wait()
    own_dw = d_w_down(wg, k)
    for h in both:
        arrived(whole(slot_l, pieces[h]), dg_recv[1][h])
        send_same(one(slot_l, 0, pieces[h]), right, dg_recv[3][h])
        send_same(rest(slot_l, pieces[h]), partner, dg_recv[8][h])
        arrived(whole(slot_r, pieces[h]), dg_recv[2][h])
        send_same(one(slot_r, 1, pieces[h]), left, dg_recv[4][h])
        send_same(rest(slot_r, pieces[h]), partner, dg_recv[9][h])
        if h == 0:
            combine()
            product(slot_l, 0)
            product(slot_r, 0)
            for slot, sem in hid_sib:
                arrived(hid.at[pl.ds(hint(slot * 2 * t, 16), 2 * t), other_half], sem)
            fetch(hid.at[:, other_half], wu.at[0:tokens]).wait()
            other_dw = d_w_down(wu, k1)
    for h in both:
        arrived(whole(slot_part, pieces[h]), dg_recv[0][h])
        send_same(most(slot_part, pieces[h]), right, dg_recv[5][h])
        send_same(most(slot_part, pieces[h]), left, dg_recv[6][h])
    product(slot_l, 1)
    product(slot_r, 1)
    for h in both:
        arrived(one(slot_f, 0, pieces[h]), dg_recv[3][h])
        arrived(one(slot_f, 1, pieces[h]), dg_recv[4][h])
        send_same(whole(slot_f, pieces[h]), partner, dg_recv[7][h])
        if h == 0:
            combine()
            product(slot_part, 0)
            product(slot_part, 1)
            combine()
        product(slot_f, h)
    combine()
    combine()

    same = lax.rem(y + b, 2)
    over_z(y)
    send(vs.at[y], dn.at[same], sum_to(y), d_sems.at[same], not_own_sum)

    @pl.when(own_sum)
    def _():
        dn[same] = vs[y]

    for h in both:
        arrived(whole(slot_fo, pieces[h]), dg_recv[7][h])
        product(slot_fo, h)
        arrived(most(slot_lo, pieces[h]), dg_recv[5][h])
        arrived(rest(slot_lo, pieces[h]), dg_recv[8][h])
        product(slot_lo, h)
        arrived(most(slot_ro, pieces[h]), dg_recv[6][h])
        arrived(rest(slot_ro, pieces[h]), dg_recv[9][h])
        product(slot_ro, h)
    combine()
    combine()
    combine()
    over_z(y1)
    send(vs.at[y1], dn.at[1 - same], sum_to(y1), d_sems.at[1 - same])

    @pl.when(not_own_sum)
    def _():
        arrived(dn.at[0], d_sems.at[0])

    arrived(dn.at[1], d_sems.at[1])
    scaled = (dn[0].astype(F32) + dn[1].astype(F32)) * gains[2]
    normed = mid[...].astype(F32) * inverse_mid_column
    inner = jnp.sum(scaled * normed, axis=1, keepdims=True)
    square[0:t, :] = jnp.broadcast_to(inner, (t, 128))
    fin[c] = jnp.transpose(square[...])[0:8, :]
    fin_recv = {}
    for step in (4, 5, 3, 6, 2, 7, 1):
        fin_recv[step] = new_recv()
        send_same(fin.at[c], (r, lax.rem(c + step, 8)), fin_recv[step])
    for step in (1, 7, 2, 6, 3, 5, 4):
        arrived(fin.at[lax.rem(c + 8 - step, 8)], fin_recv[step])
    total = fin[0]
    for i in range(1, 8):
        total = total + fin[i]
    square[0:8, :] = total
    inner_column = jnp.transpose(square[...])[0:t, 0:1]
    outv[...] = (
        outv[...].astype(F32) + inverse_mid_column * (scaled - normed * (inner_column / model))
    ).astype(BF16)
    final = fetch(outv, out_hbm)
    own_dw.wait()
    other_dw.wait()
    final.wait()
    for copy, when in sent:
        if when is None:
            copy.wait_send()
        else:
            pl.when(when)(copy.wait_send)


def local(
    block_out, stream_mid, gate_pre, up_pre, final_gain, mlp_gain, value_weight, returns, response_mask, w_gate, w_up, w_down
):
    t, width = block_out.shape
    units = gate_pre.shape[1]
    half, feat = units // 2, width // 2
    any_spec = pl.BlockSpec(memory_space=pl.ANY)
    vm = pltpu.VMEM
    out, _, d_w_down = pl.pallas_call(
        kernel,
        out_shape=(
            jax.ShapeDtypeStruct((t, width), BF16),
            jax.ShapeDtypeStruct((16 * t, units), BF16),
            jax.ShapeDtypeStruct((units, feat), BF16),
        ),
        in_specs=[any_spec] * 12,
        out_specs=(any_spec,) * 3,
        scratch_shapes=[
            vm((t, width), BF16),
            vm((t, width), BF16),
            vm((3, 1, width), F32),
            vm((1, t), F32),
            vm((1, t), jnp.int32),
            vm((8, 128), F32),
            vm((2, t, half), BF16),
            vm((2, t, half), BF16),
            vm((2, half, feat), BF16),
            vm((width, half), BF16),
            vm((width, half), BF16),
            vm((width, half), BF16),
            vm((half, width), BF16),
            vm((half, width), BF16),
            vm((2 * t, half), F32),
            vm((2 * t, half), F32),
            vm((2 * t, half), BF16),
            vm((128, 128), F32),
            vm((8, 8, 128), F32),
            vm((128, 128), F32),
            vm((2, 8, t, width), BF16),
            vm((1, width), F32),
            vm((1, width), F32),
            vm((16 * t, width), BF16),
            vm((16 * t, half), BF16),
            vm((2 * t, half), BF16),
            vm((2 * t, half), BF16),
            vm((2 * t, half), BF16),
            vm((t, half), BF16),
            vm((t, half), BF16),
            vm((2 * t, half), BF16),
            vm((2 * t, half), BF16),
            vm((2 * t, half), BF16),
            vm((8, 2, 2 * t, half), BF16),
            vm((8, 2 * t, width), F32),
            vm((8, 2 * t, width), BF16),
            vm((8, t, width), BF16),
            vm((8, t, width), BF16),
            vm((2, 4, t, width), BF16),
            vm((2, t, width), BF16),
            vm((2, t, width), BF16),
            vm((8, 8, 128), F32),
            vm((t, width), BF16),
            pltpu.SemaphoreType.DMA((N_SEND,)),
            pltpu.SemaphoreType.DMA((N_RECV,)),
            pltpu.SemaphoreType.DMA((N_LOCAL,)),
            pltpu.SemaphoreType.DMA((2, 4)),
            pltpu.SemaphoreType.DMA((2,)),
        ],
        compiler_params=pltpu.CompilerParams(
            collective_id=0, has_side_effects=True, vmem_limit_bytes=60 * 1024 * 1024
        ),
    )(
        block_out, stream_mid, gate_pre, up_pre,
        final_gain.reshape(1, width), mlp_gain.reshape(1, width), value_weight.reshape(1, width),
        returns.reshape(1, t), response_mask.reshape(1, t), w_gate, w_up, w_down,
    )
    return out, d_w_down.astype(F32)


def solution(mesh):
    placed = (
        P("row", "col"), P("row", "col"), P("row", "col"), P("row", "col"),
        P("col"), P("col"), P("col"), P("row"), P("row"),
        P("row", "col"), P("row", "col"), P("col", "row"),
    )
    return jax.shard_map(
        local, mesh=mesh, in_specs=placed, out_specs=(P("row", "col"), P("col", "row")), check_vma=False
    )
```

```python
import functools
import math

import jax
import jax.numpy as jnp
from jax import lax
from jax.experimental import pallas as pl
from jax.experimental.pallas import tpu as pltpu
from jax.sharding import PartitionSpec as P

EPSILON = 1e-05
MESH = pl.DeviceIdType.MESH
F32 = jnp.float32
BF16 = jnp.bfloat16


def dot(left, right):
    return lax.dot_general(left, right, (((1,), (0,)), ((), ())), preferred_element_type=F32)


def hint(value, factor):
    return pl.multiple_of(value, factor)


class Sems:
    def __init__(self, ref):
        self.ref, self.used = ref, 0

    def __call__(self):
        self.used += 1
        return self.ref.at[self.used - 1]


N_SEND, N_RECV, N_LOCAL = 160, 160, 24


def kernel(
    block_hbm, mid_hbm, gate_hbm, up_hbm, final_gain, mlp_gain, value_weight, returns, mask, w_gate, w_up, w_down,
    out_hbm, hid, dw_hbm,
    blk, mid, gains, ret, msk, pack, gx, ux, wd, wg, wu, wdt, wgt, wut, fa, fb, hid_own,
    square, stat, share, tile, head, head_j, dout, part_sum,
    rf, nl, nr, ha, hb, ml, mr, my, dg, yf, yb, sb, zs, zr, vs, dn, fin, outv,
    send_sems, recv_sems, local_sems, z_sems, d_sems,
):
    t, width = blk.shape
    half = gx.shape[2]
    feat = width // 2
    tokens = 16 * t
    model = 8 * width
    first = (half // 2 + 255) // 256 * 256 if half >= 512 else half // 2
    pieces = (pl.ds(0, first), pl.ds(first, half - first))
    r, c = lax.axis_index("row"), lax.axis_index("col")
    k, j = lax.rem(r, 2), lax.div(r, 2)
    x, y = lax.div(j, 2), lax.rem(j, 2)
    z, b = lax.div(c, 2), lax.rem(c, 2)
    k1, y1, b1 = 1 - k, 1 - y, 1 - b
    xr, xl, xf = lax.rem(x + 1, 4), lax.rem(x + 3, 4), lax.rem(x + 2, 4)
    zp, zm, zf = lax.rem(z + 1, 4), lax.rem(z + 3, 4), lax.rem(z + 2, 4)
    sibling = (2 * j + k1, c)
    right, left = (4 * xr + 2 * y + k, c), (4 * xl + 2 * y + k, c)
    partner = (4 * x + 2 * y1 + k, c)
    z_plus, z_minus, z_partner = (r, 2 * zp + b), (r, 2 * zm + b), (r, 2 * z + b1)
    slot_own, slot_part = 2 * x + y, 2 * x + y1
    slot_l, slot_r, slot_f = 2 * xl + y, 2 * xr + y, 2 * xf + y
    slot_lo, slot_ro, slot_fo = 2 * xl + y1, 2 * xr + y1, 2 * xf + y1
    own_half = pl.ds(hint(k * half, 128), half)
    other_half = pl.ds(hint(k1 * half, 128), half)
    diagonal = j == c
    off_diagonal = j != c
    new_send, new_recv, new_local = Sems(send_sems), Sems(recv_sems), Sems(local_sems)
    sent = []

    def send(src, dst, to, recv, when=None):
        copy = pltpu.make_async_remote_copy(
            src_ref=src, dst_ref=dst, send_sem=new_send(), recv_sem=recv, device_id=to, device_id_type=MESH
        )
        if when is None:
            copy.start()
        else:
            pl.when(when)(copy.start)
        sent.append((copy, when))

    def send_same(ref, to, recv):
        send(ref, ref, to, recv)

    def arrived(dst, recv):
        pltpu.make_async_copy(dst, dst, recv).wait()

    def fetch(src, dst):
        copy = pltpu.make_async_copy(src, dst, new_local())
        copy.start()
        return copy

    barrier = pltpu.get_barrier_semaphore()

    def greet(device):
        pl.semaphore_signal(barrier, inc=1, device_id=device, device_id_type=MESH)

    def perm_to(which):
        return (2 * c + k, 2 * x + which)

    def perm_from():
        return (2 * c + k, j)

    sum_x = lax.rem(z + 4 - x, 4)
    own_sum = jnp.logical_and(diagonal, x == 0)
    not_own_sum = jnp.logical_not(own_sum)

    def sum_to(which):
        return (2 * (2 * sum_x + which) + k, j)

    def sum_from(which):
        return (2 * c + k, 2 * lax.rem(x + z, 4) + which)

    greet(sum_to(b1))
    greet(sum_from(y1))

    @pl.when(not_own_sum)
    def _():
        greet(sum_to(b))
        greet(sum_from(y))

    @pl.when(off_diagonal)
    def _():
        greet(perm_to(y))
        greet(perm_from())

    for step in (4, 5, 3, 6, 2, 7, 1):
        greet((r, lax.rem(c + step, 8)))
    for step in (8, 9, 7, 10, 6, 11, 5, 12, 4, 13, 3, 14, 2, 15, 1):
        greet((lax.rem(r + step, 16), c))

    small = [
        fetch(block_hbm, blk),
        fetch(mid_hbm, mid),
        fetch(final_gain, gains.at[0]),
        fetch(value_weight, gains.at[1]),
        fetch(mlp_gain, gains.at[2]),
        fetch(returns, ret),
        fetch(mask, msk),
    ]
    halves = [fetch(gate_hbm.at[:, own_half], gx.at[k]), fetch(up_hbm.at[:, own_half], ux.at[k])]
    own_rows = pl.ds(hint(k * feat, 16), feat)
    weights_down = fetch(w_down.at[own_half, :], wd.at[k])
    weights_in = [fetch(w_gate.at[:, own_half], wg.at[own_rows]), fetch(w_up.at[:, own_half], wu.at[own_rows])]
    for copy in small:
        copy.wait()

    lane = lax.broadcasted_iota(jnp.int32, (t, 128), 1)
    head[...] = gains[0] * gains[1]
    block_wide = blk[...].astype(F32)
    mid_wide = mid[...].astype(F32)
    square[...] = jnp.zeros_like(square)
    pack[...] = jnp.zeros_like(pack)
    sum_out = jnp.sum(block_wide * block_wide, axis=1, keepdims=True)
    sum_head = jnp.sum(block_wide * head[...], axis=1, keepdims=True)
    sum_mid = jnp.sum(mid_wide * mid_wide, axis=1, keepdims=True)
    square[0:t, :] = jnp.where(
        lane == 0, sum_out, jnp.where(lane == 1, sum_head, jnp.where(lane == 2, sum_mid, 0.0))
    )
    stat[c] = jnp.transpose(square[...])[0:8, :]

    @pl.when(off_diagonal)
    def _():
        pl.semaphore_wait(barrier, 28)

    @pl.when(jnp.logical_and(diagonal, x != 0))
    def _():
        pl.semaphore_wait(barrier, 26)

    @pl.when(own_sum)
    def _():
        pl.semaphore_wait(barrier, 24)

    stat_recv = {}
    for step in (4, 5, 3, 6, 2, 7, 1):
        stat_recv[step] = new_recv()
        send_same(stat.at[c], (r, lax.rem(c + step, 8)), stat_recv[step])
    perm_recv, perm_head = new_recv(), new_recv()
    send(block_hbm, tile.at[k, j], perm_to(y), perm_recv, off_diagonal)
    send(head, head_j, perm_to(y), perm_head, off_diagonal)

    @pl.when(diagonal)
    def _():
        tile[k, j] = blk[...]
        head_j[...] = head[...]

    gate_recv, up_recv, wd_recv, wg_recv, wu_recv = (new_recv() for _ in range(5))
    send(gate_hbm.at[:, other_half], gx.at[k], sibling, gate_recv)
    send(up_hbm.at[:, other_half], ux.at[k], sibling, up_recv)
    send(w_down.at[other_half, :], wd.at[k], sibling, wd_recv)

    for copy in halves:
        copy.wait()
    arrived(gx.at[k1], gate_recv)
    arrived(ux.at[k1], up_recv)
    for q in range(2):

        @pl.loop(0, t // 16)
        def _(i):
            rows = pl.ds(hint(i * 16, 16), 16)
            out_rows = pl.ds(hint(q * t + i * 16, 16), 16)
            gate, up = gx[q, rows, :].astype(F32), ux[q, rows, :].astype(F32)
            sig = jax.nn.sigmoid(gate)
            silu = gate * sig
            fa[out_rows, :] = up * sig * (1.0 + gate * (1.0 - sig))
            fb[out_rows, :] = silu
            hid_own[out_rows, :] = (silu * up).astype(BF16)

    def hid_slot(slot, rows=None):
        size = 2 * t if rows is None else t
        return hid.at[pl.ds(hint(slot * 2 * t + (rows or 0), 16), size), own_half]

    hid_recv = [new_recv() for _ in range(10)]
    hid_sib = []

    def hid_to_sibling(slot):
        hid_sib.append((slot, new_recv()))
        send_same(hid_slot(slot), sibling, hid_sib[-1][1])

    own_hid = fetch(hid_own, hid_slot(slot_own))

    for step in (1, 7, 2, 6, 3, 5, 4):
        arrived(stat.at[lax.rem(c + 8 - step, 8)], stat_recv[step])
    total = stat[0]
    for i in range(1, 8):
        total = total + stat[i]
    total = total[:, 0:t]
    inverse_out = lax.rsqrt(total[0:1] / model + EPSILON)
    value = inverse_out * total[1:2]
    live = msk[...].astype(F32)
    slope = inverse_out * (live * (value - ret[...]))
    pack[0:1, 0:t] = slope
    pack[1:2, 0:t] = -slope * inverse_out * value / model
    pack[2:3, 0:t] = live
    pack[3:4, 0:t] = lax.rsqrt(total[2:3] / model + EPSILON)
    own_share = pl.ds(hint(8 * r, 8), 8)
    share[own_share, :] = pack[...]
    share_recv = {}
    for step in (8, 9, 7, 10, 6, 11, 5, 12, 4, 13, 3, 14, 2, 15, 1):
        share_recv[step] = new_recv()
        send_same(share.at[own_share], (lax.rem(r + step, 16), c), share_recv[step])

    sib_tile = []

    def tile_to_sibling(slot):
        sib_tile.append((slot, new_recv()))
        send_same(tile.at[k, slot], sibling, sib_tile[-1][1])

    t_part, t_own_m, t_own_p, t_oth_m, t_oth_p, t_far_own, t_far_oth = (new_recv() for _ in range(7))

    @pl.when(off_diagonal)
    def _():
        arrived(tile.at[k, c], perm_recv)
        arrived(head_j, perm_head)

    send_same(tile.at[k, c], z_partner, t_part)
    send_same(tile.at[k, c], z_plus, t_own_m)
    send_same(tile.at[k, c], z_minus, t_own_p)
    tile_to_sibling(c)
    send(hid_own, hid_slot(slot_own), right, hid_recv[1])
    send(hid_own, hid_slot(slot_own), left, hid_recv[2])
    send(hid_own, hid_slot(slot_own), partner, hid_recv[0])

    weights_down.wait()
    arrived(wd.at[k1], wd_recv)
    u_tile = 256 if half % 256 == 0 else 128
    for q in range(2):

        @pl.loop(0, half // u_tile)
        def _(n):
            units = pl.ds(hint(n * u_tile, 128), u_tile)
            wdt[q * feat : (q + 1) * feat, units] = jnp.transpose(wd[q, units, :])

    arrived(tile.at[k, 2 * zm + b], t_own_m)
    send_same(tile.at[k, 2 * zm + b], z_plus, t_far_own)
    tile_to_sibling(2 * zm + b)
    arrived(tile.at[k, 2 * z + b1], t_part)
    send_same(tile.at[k, 2 * z + b1], z_plus, t_oth_m)
    send_same(tile.at[k, 2 * z + b1], z_minus, t_oth_p)
    tile_to_sibling(2 * z + b1)
    arrived(tile.at[k, 2 * zp + b], t_own_p)
    tile_to_sibling(2 * zp + b)

    arrived(tile.at[k, 2 * zp + b1], t_oth_p)
    send_same(tile.at[k, 2 * zp + b1], z_minus, t_far_oth)
    tile_to_sibling(2 * zp + b1)
    arrived(hid_slot(slot_l), hid_recv[1])
    send_same(hid_slot(slot_l, 0), right, hid_recv[3])
    send_same(hid_slot(slot_l, t), partner, hid_recv[8])
    arrived(hid_slot(slot_r), hid_recv[2])
    send_same(hid_slot(slot_r, t), left, hid_recv[4])
    send_same(hid_slot(slot_r, t), partner, hid_recv[9])
    arrived(tile.at[k, 2 * zm + b1], t_oth_m)
    tile_to_sibling(2 * zm + b1)
    arrived(tile.at[k, 2 * zf + b], t_far_own)
    tile_to_sibling(2 * zf + b)

    for step in (1, 15, 2, 14, 3, 13, 4, 12, 5, 11, 6, 10, 7, 9, 8):
        from_row = lax.rem(r + 16 - step, 16)
        arrived(share.at[pl.ds(hint(8 * from_row, 8), 8)], share_recv[step])
    shares = share[...]
    which = lax.rem(lax.broadcasted_iota(jnp.int32, (128, 128), 0), 8)
    count = jnp.sum(jnp.sum(jnp.where(which == 2, shares, 0.0), axis=0, keepdims=True), axis=1, keepdims=True)
    factor = tokens * math.sqrt(model) / count
    columns = jnp.transpose(shares) * factor
    square[0:8, :] = pack[...]
    own_columns = jnp.transpose(square[...])

    arrived(tile.at[k, 2 * zf + b1], t_far_oth)
    tile_to_sibling(2 * zf + b1)
    send(w_gate.at[:, other_half], wg.at[own_rows], sibling, wg_recv)
    send(w_up.at[:, other_half], wu.at[own_rows], sibling, wu_recv)
    arrived(hid_slot(slot_part), hid_recv[0])
    send_same(hid_slot(slot_part, 0), right, hid_recv[5])
    send_same(hid_slot(slot_part, 0), left, hid_recv[6])
    for slot, sem in sib_tile:
        arrived(tile.at[k1, slot], sem)

    head_row = head_j[...]
    for s in range(8):
        for q in range(2):
            at = 8 * (2 * s + q)
            dout[(2 * s + q) * t : (2 * s + q + 1) * t, :] = (
                columns[0:t, at : at + 1] * head_row + columns[0:t, at + 1 : at + 2] * tile[q, s].astype(F32)
            ).astype(BF16)

    def chunk(slot, piece, start=0, size=2 * t):
        return part_sum.at[pl.ds(hint(slot * 2 * t + start, 16), size), piece]

    def hidden(slot, piece):
        rows = pl.ds(hint(slot * 2 * t, 16), 2 * t)
        part_sum[rows, piece] = dot(dout[rows, :], wdt[:, piece]).astype(BF16)

    def add_into(slot, piece, others, start=0, size=2 * t):
        @pl.loop(0, size // 16)
        def _(i):
            rows = pl.ds(hint(slot * 2 * t + start + i * 16, 16), 16)
            their = pl.ds(hint(i * 16, 16), 16)
            value = part_sum[rows, piece].astype(F32)
            for other in others:
                value = value + other[their, piece].astype(F32)
            part_sum[rows, piece] = value.astype(BF16)

    both = (0, 1)
    rf_s, nl_s, nr_s, ha_s, hb_s, ml_s, mr_s, my_s = ([new_recv(), new_recv()] for _ in range(8))
    for h in both:
        hidden(slot_fo, pieces[h])
        send(chunk(slot_fo, pieces[h]), rf.at[:, pieces[h]], partner, rf_s[h])
        hidden(slot_ro, pieces[h])
        send(chunk(slot_ro, pieces[h]), nl.at[:, pieces[h]], right, nl_s[h])
        hidden(slot_lo, pieces[h])
        send(chunk(slot_lo, pieces[h]), nr.at[:, pieces[h]], left, nr_s[h])
    arrived(hid_slot(slot_f, 0), hid_recv[3])
    arrived(hid_slot(slot_f, t), hid_recv[4])
    send_same(hid_slot(slot_f), partner, hid_recv[7])
    for h in both:
        hidden(slot_f, pieces[h])
        arrived(rf.at[:, pieces[h]], rf_s[h])
        add_into(slot_f, pieces[h], (rf,))
        send(chunk(slot_f, pieces[h], 0, t), ha.at[:, pieces[h]], right, ha_s[h])
        send(chunk(slot_f, pieces[h], t, t), hb.at[:, pieces[h]], left, hb_s[h])
    for h in both:
        hidden(slot_part, pieces[h])
    for h in both:
        hidden(slot_r, pieces[h])
        hidden(slot_l, pieces[h])
        arrived(nl.at[:, pieces[h]], nl_s[h])
        arrived(nr.at[:, pieces[h]], nr_s[h])
        add_into(slot_part, pieces[h], (nl, nr))
        send(chunk(slot_part, pieces[h]), my.at[:, pieces[h]], partner, my_s[h])
    for h in both:
        arrived(ha.at[:, pieces[h]], ha_s[h])
        add_into(slot_r, pieces[h], (ha,), 0, t)
        send(chunk(slot_r, pieces[h]), ml.at[:, pieces[h]], right, ml_s[h])
        arrived(hb.at[:, pieces[h]], hb_s[h])
        add_into(slot_l, pieces[h], (hb,), t, t)
        send(chunk(slot_l, pieces[h]), mr.at[:, pieces[h]], left, mr_s[h])
    for h in both:
        hidden(slot_own, pieces[h])

    own_hid.wait()
    arrived(hid_slot(slot_lo, 0), hid_recv[5])
    arrived(hid_slot(slot_ro, 0), hid_recv[6])
    arrived(hid_slot(slot_lo, t), hid_recv[8])
    arrived(hid_slot(slot_ro, t), hid_recv[9])
    arrived(hid_slot(slot_fo), hid_recv[7])
    for slot in (slot_own, slot_l, slot_r, slot_part, slot_f, slot_lo, slot_ro, slot_fo):
        hid_to_sibling(slot)
    for copy in weights_in:
        copy.wait()
    other_rows = pl.ds(hint(k1 * feat, 16), feat)
    f_tile = 256 if width % 256 == 0 else 128
    for source, target, sem in ((wg, wgt, wg_recv), (wu, wut, wu_recv)):
        arrived(source.at[other_rows], sem)

        @pl.loop(0, width // f_tile)
        def _(n):
            features = pl.ds(hint(n * f_tile, 128), f_tile)
            target[:, features] = jnp.transpose(source[features, :])

    inverse_mid_column = own_columns[0:t, 3:4]
    outv[...] = (
        (own_columns[0:t, 0:1] * factor) * head[...] + (own_columns[0:t, 1:2] * factor) * blk[...].astype(F32)
    ).astype(BF16)

    dg_recv = [[new_recv(), new_recv()] for _ in range(10)]
    sb_recv = [new_recv() for _ in range(8)]
    pending, last = [], []

    def whole(slot, piece):
        return dg.at[slot, :, :, piece]

    cut = 2 * t - 16

    def most(slot, piece):
        return dg.at[slot, :, 0:cut, piece]

    def rest(slot, piece):
        return dg.at[slot, :, cut:, piece]

    def one(slot, which, piece):
        return dg.at[slot, which, :, piece]

    for h in both:
        piece = pieces[h]
        arrived(my.at[:, piece], my_s[h])
        arrived(ml.at[:, piece], ml_s[h])
        arrived(mr.at[:, piece], mr_s[h])

        @pl.loop(0, 2 * t // 16)
        def _(i):
            rows = pl.ds(hint(i * 16, 16), 16)
            d_hidden = (
                part_sum[pl.ds(hint(slot_own * 2 * t + i * 16, 16), 16), piece].astype(F32)
                + ml[rows, piece].astype(F32)
                + mr[rows, piece].astype(F32)
                + my[rows, piece].astype(F32)
            )
            dg[slot_own, 0, rows, piece] = (d_hidden * fa[rows, piece]).astype(BF16)
            dg[slot_own, 1, rows, piece] = (d_hidden * fb[rows, piece]).astype(BF16)

        send_same(whole(slot_own, piece), right, dg_recv[1][h])
        send_same(whole(slot_own, piece), left, dg_recv[2][h])
        send_same(whole(slot_own, piece), partner, dg_recv[0][h])

    def product(slot, h):
        piece = pieces[h]
        value = dot(dg[slot, 0, :, piece], wgt[piece, :]) + dot(dg[slot, 1, :, piece], wut[piece, :])
        if h == 0:
            yf[slot] = value
            return
        value = value + yf[slot]
        yf[slot] = value
        yb[slot] = value.astype(BF16)
        sem = sb_recv[len(last) + len(pending)]
        send(yb.at[slot, pl.ds(hint(k1 * t, 16), t)], sb.at[slot], sibling, sem)
        pending.append((slot, sem))

    def combine():
        slot, sem = pending.pop(0)
        arrived(sb.at[slot], sem)
        zz, bb = lax.rem(lax.div(slot, 2) + x, 4), lax.rem(slot, 2)
        summed = (yf[slot, pl.ds(hint(k * t, 16), t), :] + sb[slot].astype(F32)).astype(BF16)
        zs[slot] = summed
        send(zs.at[slot], zr.at[bb, z], (r, 2 * zz + b), z_sems.at[bb, z], zz != z)

        @pl.when(zz == z)
        def _():
            zr[bb, z] = summed

        last.append(slot)

    def over_z(q):
        for step in range(1, 4):
            zz = lax.rem(z + step, 4)
            arrived(zr.at[q, zz], z_sems.at[q, zz])
        vs[q] = (
            zr[q, 0].astype(F32) + zr[q, 1].astype(F32) + zr[q, 2].astype(F32) + zr[q, 3].astype(F32)
        ).astype(BF16)

    def d_w_down(source, part):
        @pl.loop(0, half // u_tile)
        def _(n):
            units = pl.ds(hint(n * u_tile, 128), u_tile)
            wd[part, units, :] = lax.dot_general(
                source[0:tokens, units],
                dout[:, pl.ds(hint(k * feat, 128), feat)],
                (((0,), (0,)), ((), ())),
                preferred_element_type=F32,
            ).astype(BF16)

        part_rows = pl.ds(hint(part * half, 16), half)
        return fetch(wd.at[part], dw_hbm.at[part_rows, :])

    product(slot_own, 0)
    product(slot_own, 1)
    fetch(hid.at[:, own_half], wg.at[0:tokens]).wait()
    own_dw = d_w_down(wg, k)
    for h in both:
        arrived(whole(slot_l, pieces[h]), dg_recv[1][h])
        send_same(one(slot_l, 0, pieces[h]), right, dg_recv[3][h])
        send_same(rest(slot_l, pieces[h]), partner, dg_recv[8][h])
        arrived(whole(slot_r, pieces[h]), dg_recv[2][h])
        send_same(one(slot_r, 1, pieces[h]), left, dg_recv[4][h])
        send_same(rest(slot_r, pieces[h]), partner, dg_recv[9][h])
        if h == 0:
            combine()
            product(slot_l, 0)
            product(slot_r, 0)
            for slot, sem in hid_sib:
                arrived(hid.at[pl.ds(hint(slot * 2 * t, 16), 2 * t), other_half], sem)
            fetch(hid.at[:, other_half], wu.at[0:tokens]).wait()
            other_dw = d_w_down(wu, k1)
    for h in both:
        arrived(whole(slot_part, pieces[h]), dg_recv[0][h])
        send_same(most(slot_part, pieces[h]), right, dg_recv[5][h])
        send_same(most(slot_part, pieces[h]), left, dg_recv[6][h])
    product(slot_l, 1)
    product(slot_r, 1)
    for h in both:
        arrived(one(slot_f, 0, pieces[h]), dg_recv[3][h])
        arrived(one(slot_f, 1, pieces[h]), dg_recv[4][h])
        send_same(whole(slot_f, pieces[h]), partner, dg_recv[7][h])
        if h == 0:
            combine()
            product(slot_part, 0)
            product(slot_part, 1)
            combine()
        product(slot_f, h)
    combine()
    combine()

    same = lax.rem(y + b, 2)
    over_z(y)
    send(vs.at[y], dn.at[same], sum_to(y), d_sems.at[same], not_own_sum)

    @pl.when(own_sum)
    def _():
        dn[same] = vs[y]

    for h in both:
        arrived(whole(slot_fo, pieces[h]), dg_recv[7][h])
        product(slot_fo, h)
        arrived(most(slot_lo, pieces[h]), dg_recv[5][h])
        arrived(rest(slot_lo, pieces[h]), dg_recv[8][h])
        product(slot_lo, h)
        if h == 1:
            combine()
        arrived(most(slot_ro, pieces[h]), dg_recv[6][h])
        arrived(rest(slot_ro, pieces[h]), dg_recv[9][h])
        product(slot_ro, h)
    combine()
    combine()
    over_z(y1)
    send(vs.at[y1], dn.at[1 - same], sum_to(y1), d_sems.at[1 - same])

    @pl.when(not_own_sum)
    def _():
        arrived(dn.at[0], d_sems.at[0])

    arrived(dn.at[1], d_sems.at[1])
    scaled = (dn[0].astype(F32) + dn[1].astype(F32)) * gains[2]
    normed = mid[...].astype(F32) * inverse_mid_column
    inner = jnp.sum(scaled * normed, axis=1, keepdims=True)
    square[0:t, :] = jnp.broadcast_to(inner, (t, 128))
    fin[c] = jnp.transpose(square[...])[0:8, :]
    fin_recv = {}
    for step in (4, 5, 3, 6, 2, 7, 1):
        fin_recv[step] = new_recv()
        send_same(fin.at[c], (r, lax.rem(c + step, 8)), fin_recv[step])
    for step in (1, 7, 2, 6, 3, 5, 4):
        arrived(fin.at[lax.rem(c + 8 - step, 8)], fin_recv[step])
    total = fin[0]
    for i in range(1, 8):
        total = total + fin[i]
    square[0:8, :] = total
    inner_column = jnp.transpose(square[...])[0:t, 0:1]
    outv[...] = (
        outv[...].astype(F32) + inverse_mid_column * (scaled - normed * (inner_column / model))
    ).astype(BF16)
    final = fetch(outv, out_hbm)
    own_dw.wait()
    other_dw.wait()
    final.wait()
    for copy, when in sent:
        if when is None:
            copy.wait_send()
        else:
            pl.when(when)(copy.wait_send)


def local(
    block_out, stream_mid, gate_pre, up_pre, final_gain, mlp_gain, value_weight, returns, response_mask, w_gate, w_up, w_down
):
    t, width = block_out.shape
    units = gate_pre.shape[1]
    half, feat = units // 2, width // 2
    any_spec = pl.BlockSpec(memory_space=pl.ANY)
    vm = pltpu.VMEM
    out, _, d_w_down = pl.pallas_call(
        kernel,
        out_shape=(
            jax.ShapeDtypeStruct((t, width), BF16),
            jax.ShapeDtypeStruct((16 * t, units), BF16),
            jax.ShapeDtypeStruct((units, feat), BF16),
        ),
        in_specs=[any_spec] * 12,
        out_specs=(any_spec,) * 3,
        scratch_shapes=[
            vm((t, width), BF16),
            vm((t, width), BF16),
            vm((3, 1, width), F32),
            vm((1, t), F32),
            vm((1, t), jnp.int32),
            vm((8, 128), F32),
            vm((2, t, half), BF16),
            vm((2, t, half), BF16),
            vm((2, half, feat), BF16),
            vm((width, half), BF16),
            vm((width, half), BF16),
            vm((width, half), BF16),
            vm((half, width), BF16),
            vm((half, width), BF16),
            vm((2 * t, half), F32),
            vm((2 * t, half), F32),
            vm((2 * t, half), BF16),
            vm((128, 128), F32),
            vm((8, 8, 128), F32),
            vm((128, 128), F32),
            vm((2, 8, t, width), BF16),
            vm((1, width), F32),
            vm((1, width), F32),
            vm((16 * t, width), BF16),
            vm((16 * t, half), BF16),
            vm((2 * t, half), BF16),
            vm((2 * t, half), BF16),
            vm((2 * t, half), BF16),
            vm((t, half), BF16),
            vm((t, half), BF16),
            vm((2 * t, half), BF16),
            vm((2 * t, half), BF16),
            vm((2 * t, half), BF16),
            vm((8, 2, 2 * t, half), BF16),
            vm((8, 2 * t, width), F32),
            vm((8, 2 * t, width), BF16),
            vm((8, t, width), BF16),
            vm((8, t, width), BF16),
            vm((2, 4, t, width), BF16),
            vm((2, t, width), BF16),
            vm((2, t, width), BF16),
            vm((8, 8, 128), F32),
            vm((t, width), BF16),
            pltpu.SemaphoreType.DMA((N_SEND,)),
            pltpu.SemaphoreType.DMA((N_RECV,)),
            pltpu.SemaphoreType.DMA((N_LOCAL,)),
            pltpu.SemaphoreType.DMA((2, 4)),
            pltpu.SemaphoreType.DMA((2,)),
        ],
        compiler_params=pltpu.CompilerParams(
            collective_id=0, has_side_effects=True, vmem_limit_bytes=60 * 1024 * 1024
        ),
    )(
        block_out, stream_mid, gate_pre, up_pre,
        final_gain.reshape(1, width), mlp_gain.reshape(1, width), value_weight.reshape(1, width),
        returns.reshape(1, t), response_mask.reshape(1, t), w_gate, w_up, w_down,
    )
    return out, d_w_down.astype(F32)


def solution(mesh):
    placed = (
        P("row", "col"), P("row", "col"), P("row", "col"), P("row", "col"),
        P("col"), P("col"), P("col"), P("row"), P("row"),
        P("row", "col"), P("row", "col"), P("col", "row"),
    )
    return jax.shard_map(
        local, mesh=mesh, in_specs=placed, out_specs=(P("row", "col"), P("col", "row")), check_vma=False
    )
```
